512 devices in a mesh: dx: 4 (over x), dy: 16 (over z, core), solid: 8 (over y).
Axes of the slice: x: 4, y: 8, z: 8, core: 2. Of those that a mesh axis runs over, the one named last changes fastest.
Arguments:
- velocity: float32 [3, 4, 4, 4, 4, 64, 1024], P(None, None, None, None, 'dx', 'dy', 'solid'), may hold values from -6 to 6
- viscosity: float32 [4, 64, 1024], P('dx', 'dy', 'solid'), may hold values from 0.5 to 4
- cell_config: int32 [4, 64, 1024], P('dx', 'dy', 'solid'), may hold values from 0 to 7
- constraint_offsets: float32 [8, 64, 64], replicated, may hold values from -0.24 to 0.24
- slot_cells: int32 [4, 128, 1024], P('dx', ('dy', 'solid')), may hold values from -1 to 511, as said below
- point_coords: float32 [3, 4, 128, 1024], P(None, 'dx', ('dy', 'solid')), may hold values from 0 to 1
- strain_offsets: float32 [3, 3, 4, 128, 1024], P(None, None, 'dx', ('dy', 'solid')), may hold values from -1.5 to 1.5
- solid_velocity: float32 [3, 4, 128, 1024], P(None, 'dx', ('dy', 'solid')), may hold values from -6 to 6
Outputs:
- fluid_out: float32 [3, 4, 4, 4, 4, 64, 1024], P(None, None, None, None, 'dx', 'dy', 'solid')
- new_deform: float32 [3, 3, 4, 128, 1024], P(None, None, 'dx', ('dy', 'solid'))
The draws below stay inside these ranges and needn't reach their ends.
Inputs may be any that keep to these rules, and one draw needn't show every extreme that they name: `slot_cells`: an entry is -1 for an empty slot, else a cell of the owner numbered with x slowest and z fastest. Slots h * 8 to (h + 1) * 8 - 1 of owner o hold the points that device h keeps.
All inputs are finite; a program needn't handle non-finite values.
Results may differ from the reference program's by a relative error of at most 0.0003.
Values sent between devices are 32-bit elements; how exact they have to be, the bound alone decides.
A program may use at most 64 MiB of HBM per device.

```python
import math
import jax
import jax.numpy as jnp
import numpy as np
from jax import lax

CX = 1
CY = 4
CZ = 128
CAP = 8
NCONF = 8
GROUP = 128
SLOTS = 1024
CELLS = 512
NCX = 4
NCY = 64
NCZ = 1024
N_DX = 4
N_DY = 16
N_SOLID = 8


def draw_slot_cells(key, part):
    keys = jax.random.split(jax.random.fold_in(key, 11), 5)
    cells = jax.random.randint(keys[0], (N_DX, GROUP, SLOTS), 0, CELLS)
    level = jax.random.randint(keys[1], (N_DX, GROUP, 1), 2, 9)
    roll = jax.random.randint(keys[2], (N_DX, GROUP, SLOTS), 0, 8)
    live = roll < level
    full_owner = jax.random.randint(keys[3], (N_DX, 1, 1), 0, GROUP)
    full_holder = jax.random.randint(keys[4], (N_DX, 1, 1), 0, GROUP)
    owners = jnp.arange(GROUP)[None, :, None]
    slots = jnp.arange(SLOTS)[None, None, :]
    in_full = (owners == full_owner) & (slots // CAP == full_holder)
    live = live | in_full
    empty_one = (owners == (full_owner + 1) % GROUP) & (slots == 0)
    live = live & jnp.logical_not(empty_one)
    top_one = (owners == full_owner) & (slots == full_holder * CAP)
    cells = jnp.where(top_one, CELLS - 1, cells)
    return jnp.where(live, cells, -1).astype(jnp.int32)


def touch_ends(values, rng, low, top_value):
    longest = values.shape.index(max(values.shape))
    spots = []
    for shift in (0, 1):
        where = [jax.random.randint(jax.random.fold_in(rng, axis), (), 0, length) for axis, length in enumerate(values.shape)]
        where[longest] = (where[longest] + shift) % values.shape[longest]
        spots.append(tuple(where))
    return values.at[spots[0]].set(low).at[spots[1]].set(top_value)


def levels(own_key, dims, pieces, low, top_value):
    gain, own = 1.0, jax.random.fold_in(own_key, 6)
    for position, shards_of in pieces:
        draws = jnp.exp(jax.random.uniform(jax.random.fold_in(own, position), (shards_of,), jnp.float32, low / len(pieces), top_value / len(pieces)))
        gain = gain * jnp.repeat(draws, dims[position] // shards_of).reshape([-1 if axis == position else 1 for axis in range(len(dims))])
    return gain


def gaussian(key, extent, width, reach, cuts=(), kind=jnp.bfloat16):
    gain = levels(key, extent, cuts, -0.22, 0.18) if cuts else 1.0
    drawn = jax.random.normal(key, extent, jnp.float32) * width * gain
    return jnp.minimum(jnp.maximum(drawn, -reach), reach).astype(kind)


def setup_inputs(seed: int = 0) -> dict:
    seeds = jax.random.split(jax.random.key(seed), 9)
    velocity = gaussian(seeds[0], (3, 4, 4, 4, NCX, NCY, NCZ), 1.0, 6.0, ((4, 4), (5, 16), (6, 8)), jnp.float32)
    viscosity = jnp.clip(jnp.exp(math.log(4.0) - 2.0794415 * jax.random.uniform(seeds[1], (NCX, NCY, NCZ), jnp.float32) ** levels(seeds[1], (NCX, NCY, NCZ), ((0, 4), (1, 16), (2, 8)), -0.2, 0.2)), 0.5, 4.0)
    cell_config = touch_ends(jax.random.randint(seeds[2], (NCX, NCY, NCZ), 0, NCONF), jax.random.fold_in(seeds[2], 1), 0, NCONF - 1).astype(jnp.int32)
    constraint_offsets = gaussian(seeds[3], (NCONF, 64, 64), 0.04, 0.24, (), jnp.float32)
    slot_cells = draw_slot_cells(jax.random.fold_in(seeds[8], 71), 0)
    point_coords = jnp.clip(1.0 * jax.random.uniform(seeds[5], (3, N_DX, GROUP, SLOTS), jnp.float32) ** levels(seeds[5], (3, N_DX, GROUP, SLOTS), ((1, 4), (2, 128)), -0.2, 0.2), 0.0, 1.0)
    strain_offsets = gaussian(seeds[6], (3, 3, N_DX, GROUP, SLOTS), 0.3, 1.5, ((2, 4), (3, 128)), jnp.float32)
    solid_velocity = gaussian(seeds[7], (3, N_DX, GROUP, SLOTS), 1.0, 6.0, ((1, 4), (2, 128)), jnp.float32)
    return dict(velocity=velocity, viscosity=viscosity, cell_config=cell_config, constraint_offsets=constraint_offsets, slot_cells=slot_cells, point_coords=point_coords, strain_offsets=strain_offsets, solid_velocity=solid_velocity)


PRECISE = lax.Precision.HIGHEST
TIME_STEP = 0.05
SPRING_RATE = 2.0
PENALTY = 4.0
STIFFNESS = np.array([[2.0, -1.0, 0.0, 0.0], [-1.0, 2.0, -1.0, 0.0], [0.0, -1.0, 2.0, -1.0], [0.0, 0.0, -1.0, 2.0]])
NODE_POINTS = (0.0, 1.0 / 3.0, 2.0 / 3.0, 1.0)


def lagrange(coord):
    values = []
    slopes = []
    for which in range(4):
        others = [NODE_POINTS[j] for j in range(4) if j != which]
        denom = 1.0
        for other in others:
            denom = denom * (NODE_POINTS[which] - other)
        first = coord - others[0]
        second = coord - others[1]
        third = coord - others[2]
        values.append(first * second * third / denom)
        slopes.append((second * third + first * third + first * second) / denom)
    return jnp.stack(values), jnp.stack(slopes)


def constrain(flat, config, offsets, transpose):
    eye = jnp.eye(64, dtype=flat.dtype)
    result = jnp.zeros_like(flat)
    for which in range(NCONF):
        matrix = eye + offsets[which]
        form = 'ji,mjn->min' if transpose else 'ij,mjn->min'
        product = jnp.einsum(form, matrix, flat, precision=PRECISE)
        result = result + jnp.where(config == which, product, 0.0)
    return result


def operate(field, padded, viscosity):
    stiff = jnp.asarray(STIFFNESS, field.dtype)
    lap = jnp.einsum('ia,kabcxyz->kibcxyz', stiff, field, precision=PRECISE)
    lap = lap + jnp.einsum('ib,kabcxyz->kaicxyz', stiff, field, precision=PRECISE)
    lap = lap + jnp.einsum('ic,kabcxyz->kabixyz', stiff, field, precision=PRECISE)
    result = field + viscosity * lap
    lower_x = padded[:, :, :, :, :-2, 1:-1, 1:-1]
    upper_x = padded[:, :, :, :, 2:, 1:-1, 1:-1]
    result = result.at[:, 0].add(PENALTY * (field[:, 0] - lower_x[:, 3]))
    result = result.at[:, 3].add(PENALTY * (field[:, 3] - upper_x[:, 0]))
    lower_y = padded[:, :, :, :, 1:-1, :-2, 1:-1]
    upper_y = padded[:, :, :, :, 1:-1, 2:, 1:-1]
    result = result.at[:, :, 0].add(PENALTY * (field[:, :, 0] - lower_y[:, :, 3]))
    result = result.at[:, :, 3].add(PENALTY * (field[:, :, 3] - upper_y[:, :, 0]))
    lower_z = padded[:, :, :, :, 1:-1, 1:-1, :-2]
    upper_z = padded[:, :, :, :, 1:-1, 1:-1, 2:]
    result = result.at[:, :, :, 0].add(PENALTY * (field[:, :, :, 0] - lower_z[:, :, :, 3]))
    result = result.at[:, :, :, 3].add(PENALTY * (field[:, :, :, 3] - upper_z[:, :, :, 0]))
    return result


def evaluate(gathered, coords):
    field = gathered.reshape(3, 4, 4, 4, -1)
    value_x, slope_x = lagrange(coords[0])
    value_y, slope_y = lagrange(coords[1])
    value_z, slope_z = lagrange(coords[2])
    along_zp = jnp.einsum('kabcs,cs->kabs', field, value_z, precision=PRECISE)
    along_zd = jnp.einsum('kabcs,cs->kabs', field, slope_z, precision=PRECISE)
    plain = jnp.einsum('kabs,bs->kas', along_zp, value_y, precision=PRECISE)
    dery = jnp.einsum('kabs,bs->kas', along_zp, slope_y, precision=PRECISE)
    derz = jnp.einsum('kabs,bs->kas', along_zd, value_y, precision=PRECISE)
    vel = jnp.einsum('kas,as->ks', plain, value_x, precision=PRECISE)
    grad_x = jnp.einsum('kas,as->ks', plain, slope_x, precision=PRECISE)
    grad_y = jnp.einsum('kas,as->ks', dery, value_x, precision=PRECISE)
    grad_z = jnp.einsum('kas,as->ks', derz, value_x, precision=PRECISE)
    return vel, jnp.stack([grad_x, grad_y, grad_z], axis=1)


def solid_update(vel, grad, strain, motion):
    eye = jnp.eye(3, dtype=strain.dtype)[:, :, None]
    deform = eye + strain
    moved = deform + TIME_STEP * jnp.einsum('kjs,jls->kls', grad, deform, precision=PRECISE)
    stress = jnp.einsum('kls,mls->kms', moved, moved, precision=PRECISE) - eye
    drag = SPRING_RATE * (motion - vel)
    return moved, stress, drag


def spread_nodes(stress, drag, coords):
    value_x, slope_x = lagrange(coords[0])
    value_y, slope_y = lagrange(coords[1])
    value_z, slope_z = lagrange(coords[2])
    shape_x = jnp.einsum('as,bs,cs->abcs', slope_x, value_y, value_z, precision=PRECISE)
    shape_y = jnp.einsum('as,bs,cs->abcs', value_x, slope_y, value_z, precision=PRECISE)
    shape_z = jnp.einsum('as,bs,cs->abcs', value_x, value_y, slope_z, precision=PRECISE)
    whole = jnp.einsum('as,bs,cs->abcs', value_x, value_y, value_z, precision=PRECISE)
    nodal = jnp.einsum('ks,abcs->kabcs', stress[:, 0], shape_x, precision=PRECISE)
    nodal = nodal + jnp.einsum('ks,abcs->kabcs', stress[:, 1], shape_y, precision=PRECISE)
    nodal = nodal + jnp.einsum('ks,abcs->kabcs', stress[:, 2], shape_z, precision=PRECISE)
    nodal = jnp.einsum('ks,abcs->kabcs', drag, whole, precision=PRECISE) - nodal
    return nodal.reshape(192, -1)


def slot_work(items):
    block, targets, coords, strain, motion = items
    live = targets >= 0
    safe = jnp.where(live, targets, 0).astype(jnp.int32)
    gathered = jnp.where(live[None, :], jnp.take(block, safe, axis=1), 0.0)
    vel, grad = evaluate(gathered, coords)
    moved, stress, drag = solid_update(vel, grad, strain, motion)
    nodal = jnp.where(live[None, :], spread_nodes(stress, drag, coords), 0.0)
    force = jnp.zeros_like(block).at[:, safe].add(nodal)
    return force, moved


def reference(velocity, viscosity, cell_config, constraint_offsets, slot_cells, point_coords, strain_offsets, solid_velocity):
    shape = velocity.shape
    count = NCX * NCY * NCZ
    config = cell_config.reshape(count)
    flat = constrain(velocity.reshape(3, 64, count), config, constraint_offsets, False)
    constrained = flat.reshape(shape)
    padded = jnp.pad(constrained, ((0, 0), (0, 0), (0, 0), (0, 0), (1, 1), (1, 1), (1, 1)))
    applied = operate(constrained, padded, viscosity)
    owned = constrained.reshape(3, 4, 4, 4, N_DX, CX, N_DY, CY, N_SOLID, CZ)
    owned = owned.transpose(4, 6, 8, 0, 1, 2, 3, 5, 7, 9).reshape(N_DX * GROUP, 192, CELLS)
    targets = slot_cells.reshape(N_DX * GROUP, SLOTS)
    coords = point_coords.transpose(1, 2, 0, 3).reshape(N_DX * GROUP, 3, SLOTS)
    strain = strain_offsets.reshape(3, 3, N_DX, GROUP, GROUP, CAP).transpose(2, 4, 0, 1, 3, 5)
    strain = strain.reshape(N_DX * GROUP, 3, 3, SLOTS)
    motion = solid_velocity.reshape(3, N_DX, GROUP, GROUP, CAP).transpose(1, 3, 0, 2, 4)
    motion = motion.reshape(N_DX * GROUP, 3, SLOTS)
    force, moved = lax.map(slot_work, (owned, targets, coords, strain, motion))
    force = force.reshape(N_DX, N_DY, N_SOLID, 3, 4, 4, 4, CX, CY, CZ)
    force = force.transpose(3, 4, 5, 6, 0, 7, 1, 8, 2, 9).reshape(3, 64, count)
    total = applied.reshape(3, 64, count) - force
    fluid_out = constrain(total, config, constraint_offsets, True).reshape(shape)
    new_deform = moved.reshape(N_DX, GROUP, 3, 3, GROUP, CAP).transpose(2, 3, 0, 4, 1, 5)
    new_deform = new_deform.reshape(3, 3, N_DX, GROUP, SLOTS)
    return fluid_out, new_deform
```

```python
import jax
import jax.numpy as jnp
from jax import lax
from jax.experimental import pallas as pl
from jax.experimental.pallas import tpu as pltpu
from jax.sharding import PartitionSpec as P

F32 = jnp.float32
BF16 = jnp.bfloat16
TIME_STEP = 0.05
SPRING_RATE = 2.0
PENALTY = 4.0
NODE_POINTS = (0.0, 1.0 / 3.0, 2.0 / 3.0, 1.0)
N_DX, N_DY, N_SOLID = 4, 16, 8
MESH = pl.DeviceIdType.MESH


def iota(shape, dim):
    return lax.broadcasted_iota(jnp.int32, shape, dim)


def split(x):
    high = x.astype(BF16)
    return high, (x - high.astype(F32)).astype(BF16)


def dot(a, b):
    return lax.dot_general(a, b, (((1,), (0,)), ((), ())), preferred_element_type=F32)


def dot_nt(a, b):
    return lax.dot_general(a, b, (((1,), (1,)), ((), ())), preferred_element_type=F32)


def lagrange(coord):
    values = []
    slopes = []
    for which in range(4):
        others = [NODE_POINTS[j] for j in range(4) if j != which]
        denom = 1.0
        for other in others:
            denom = denom * (NODE_POINTS[which] - other)
        first = coord - others[0]
        second = coord - others[1]
        third = coord - others[2]
        scale = 1.0 / denom
        values.append(first * second * third * scale)
        slopes.append((second * third + first * third + first * second) * scale)
    return values, slopes


def pick(rows, index):
    out = jnp.where(index == 0, rows[0], rows[1])
    return jnp.where(index < 2, out, jnp.where(index == 2, rows[2], rows[3]))


def stiffness():
    row, col = iota((64, 64), 0), iota((64, 64), 1)
    total = jnp.where(row == col, 6.0, 0.0)
    for step in (16, 4, 1):
        place_row, place_col = (row // step) % 4, (col // step) % 4
        same = (row - place_row * step) == (col - place_col * step)
        near = jnp.abs(place_row - place_col) == 1
        total = total - jnp.where(same & near, 1.0, 0.0)
    return total


def left_operand(stack):
    high, low = split(stack)
    return jnp.concatenate([high, high, low], axis=1)


def constrain(field, left, config):
    high, low = split(field)
    product = dot(left, jnp.concatenate([high, low, high], axis=0))
    total = field
    for which in range(8):
        total = total + jnp.where(config == which, product[which * 64 : which * 64 + 64], 0.0)
    return total


def kernel(
    vel_hbm, visc_hbm, config_hbm, offsets_hbm, cells_hbm, coords_hbm, strain_hbm, motion_hbm,
    fluid_hbm, deform_hbm,
    vel, visc, config, offsets, cells, items,
    field, halves, applied, onehot, shapes, nodal, results, turned,
    packet, middle, arrived, reply, reply_middle, reply_arrived, reply_turned,
    edge, low_x, high_x, low_y, high_y, low_z, high_z,
    fluid, deform,
    in_sem, own_sem, out_sem,
    send_a, recv_a, send_b, recv_b, send_c, recv_c, send_d, recv_d, send_h, recv_h,
):
    me_x, me_y, me_s = lax.axis_index("dx"), lax.axis_index("dy"), lax.axis_index("solid")

    loads = [
        pltpu.make_async_copy(source, target, in_sem.at[which])
        for which, (source, target) in enumerate(
            (
                (strain_hbm, items.at[0:72]),
                (motion_hbm, items.at[72:96]),
                (coords_hbm, items.at[96:120]),
                (cells_hbm, cells),
                (vel_hbm, vel),
                (offsets_hbm, offsets),
                (config_hbm, config),
                (visc_hbm, visc),
            )
        )
    ]
    for load in loads:
        load.start()

    barrier = pltpu.get_barrier_semaphore()
    for step in range(1, N_SOLID):
        pl.semaphore_signal(barrier, inc=1, device_id={"solid": lax.rem(me_s + step, N_SOLID)}, device_id_type=MESH)
    for step in range(1, N_DY):
        pl.semaphore_signal(barrier, inc=1, device_id={"dy": lax.rem(me_y + step, N_DY)}, device_id_type=MESH)
    for step in (1, N_DX - 1):
        pl.semaphore_signal(barrier, inc=1, device_id={"dx": lax.rem(me_x + step, N_DX)}, device_id_type=MESH)

    def over_solid(source, target, send, recv, own):
        copies = [pltpu.make_async_copy(source.at[:, me_s], target.at[:, me_s], own)]
        for step in range(1, N_SOLID):
            peer = lax.rem(me_s + step, N_SOLID)
            copies.append(
                pltpu.make_async_remote_copy(
                    src_ref=source.at[:, peer],
                    dst_ref=target.at[:, me_s],
                    send_sem=send.at[step - 1],
                    recv_sem=recv.at[step - 1],
                    device_id={"solid": peer},
                    device_id_type=MESH,
                )
            )
        return copies

    def over_dy(source, target, send, recv, own):
        copies = [pltpu.make_async_copy(source.at[me_y], target.at[me_y], own)]
        for step in range(1, N_DY):
            peer = lax.rem(me_y + step, N_DY)
            copies.append(
                pltpu.make_async_remote_copy(
                    src_ref=source.at[peer],
                    dst_ref=target.at[me_y],
                    send_sem=send.at[step - 1],
                    recv_sem=recv.at[step - 1],
                    device_id={"dy": peer},
                    device_id_type=MESH,
                )
            )
        return copies

    def start(copies):
        for copy in copies:
            copy.start()

    def arrive(copies):
        copies[0].wait()
        for copy in copies[1:]:
            copy.wait_recv()

    slot_place = iota((1, 1024), 1) & 7
    for load in loads[:4]:
        load.wait()
    items[120:128, :] = cells[...].astype(F32)
    rows = jnp.concatenate([items[pl.ds(g, 16, stride=8), :] for g in range(8)], axis=1)
    spread = jnp.concatenate([jnp.where(slot_place == c, rows, 0.0) for c in range(8)], axis=0)
    spread_high, spread_low = split(spread)
    slot_device = jnp.where((iota((1024, 128), 0) >> 3) == iota((1024, 128), 1), 1.0, 0.0).astype(BF16)
    packed = dot(spread_high, slot_device) + dot(spread_low, slot_device)
    packet[...] = packed.T.reshape(16, 8, 128)
    turned[...] = packed
    reply_turned[...] = jnp.zeros_like(reply_turned)

    pl.semaphore_wait(barrier, N_SOLID - 1 + N_DY - 1 + 2)
    first = over_solid(packet, middle, send_a, recv_a, own_sem.at[0])
    start(first)

    for load in loads[4:]:
        load.wait()
    own_config = config[...]
    config_row = jnp.concatenate([own_config[y : y + 1] for y in range(4)], axis=1)
    left = left_operand(offsets[...].reshape(512, 64))
    for k in range(3):
        start_field = jnp.concatenate([vel[pl.ds(k * 256 + y, 64, stride=4), :] for y in range(4)], axis=1)
        own = constrain(start_field, left, config_row)
        field[k] = own.reshape(4, 16, 512)
        high, low = split(own)
        halves[k * 64 : k * 64 + 64] = high
        halves[192 + k * 64 : 192 + k * 64 + 64] = low

    def remote(source, target, which, where):
        return pltpu.make_async_remote_copy(
            src_ref=source, dst_ref=target, send_sem=send_h.at[which], recv_sem=recv_h.at[which],
            device_id=where, device_id_type=MESH,
        )

    up_x, down_x = lax.rem(me_x + 1, N_DX), lax.rem(me_x + N_DX - 1, N_DX)
    up_y, down_y = lax.rem(me_y + 1, N_DY), lax.rem(me_y + N_DY - 1, N_DY)
    up_s, down_s = lax.rem(me_s + 1, N_SOLID), lax.rem(me_s + N_SOLID - 1, N_SOLID)
    halo = [
        remote(field.at[:, 3], low_x, 0, {"dx": up_x}),
        remote(field.at[:, 0], high_x, 1, {"dx": down_x}),
        remote(field.at[:, :, 8:16, 384:512], low_y, 2, {"dy": up_y}),
        remote(field.at[:, :, 0:8, 0:128], high_y, 3, {"dy": down_y}),
        remote(edge.at[0], low_z, 4, {"solid": up_s}),
        remote(edge.at[1], high_z, 5, {"solid": down_s}),
    ]
    edge_row, edge_col = iota((16, 512), 0), iota((16, 512), 1)
    lane_edge = jnp.where(edge_row < 8, 127, 0)
    edge_pick = jnp.where(
        (edge_col == (edge_row & 7) * 128 + lane_edge) & ((edge_row & 7) < 4), 1.0, 0.0
    ).astype(BF16)
    edges = dot_nt(edge_pick, halves[0:192]) + dot_nt(edge_pick, halves[192:384])
    edge[...] = edges.reshape(2, 8, 192)

    arrive(first)
    second = over_dy(middle, arrived, send_b, recv_b, own_sem.at[1])
    start(second)
    start(halo)

    points = [turned[pl.ds(12 + j, 8, stride=16), :] for j in range(3)]
    target = turned[pl.ds(15, 8, stride=16), :]
    polys = [lagrange(point) for point in points]
    cell_index = iota((512, 256), 0).astype(F32)
    node_row = iota((16, 256), 0)
    for pair in range(4):
        lanes = slice(pair * 256, pair * 256 + 256)

        def row(x):
            return jnp.concatenate([x[2 * pair : 2 * pair + 1], x[2 * pair + 1 : 2 * pair + 2]], axis=1)

        onehot[:, lanes] = jnp.where(cell_index == row(target), 1.0, 0.0).astype(BF16)
        value_x, slope_x = [[row(x) for x in part] for part in polys[0]]
        value_y, slope_y = [pick([row(x) for x in part], node_row >> 2) for part in polys[1]]
        value_z, slope_z = [pick([row(x) for x in part], node_row & 3) for part in polys[2]]
        plain, along_y, along_z = value_y * value_z, slope_y * value_z, value_y * slope_z
        for a in range(4):
            at = slice(a * 16, a * 16 + 16)
            shapes[0, at, lanes] = value_x[a] * plain
            shapes[1, at, lanes] = slope_x[a] * plain
            shapes[2, at, lanes] = value_x[a] * along_y
            shapes[3, at, lanes] = value_x[a] * along_z
        gathered = dot(halves[...], onehot[:, lanes])
        for k in range(3):
            nodes = gathered[k * 64 : k * 64 + 64] + gathered[192 + k * 64 : 192 + k * 64 + 64]
            for j in range(4):
                total = jnp.sum(nodes * shapes[j, :, lanes], axis=0, keepdims=True)
                line = (k * 4 + j) * 8 + 2 * pair
                results[line : line + 1, :] = total[:, :128]
                results[line + 1 : line + 2, :] = total[:, 128:]

    own_visc = visc[...]
    visc_row = jnp.concatenate([own_visc[y : y + 1] for y in range(4)], axis=1)
    stiff = stiffness().astype(BF16)
    stiff = jnp.concatenate([stiff, stiff], axis=1)
    node = iota((64, 512), 0)
    ends = jnp.zeros((64, 512), F32)
    for step in (16, 4, 1):
        place = (node // step) % 4
        ends = ends + jnp.where((place == 0) | (place == 3), PENALTY, 0.0)
    for k in range(3):
        both = jnp.concatenate([halves[k * 64 : k * 64 + 64], halves[192 + k * 64 : 192 + k * 64 + 64]], axis=0)
        own = field[k].reshape(64, 512)
        applied[k] = (own * (1.0 + ends) + visc_row * dot(stiff, both)).reshape(4, 16, 512)

    arrive(second)
    mine = arrived[...].reshape(128, 128).T
    turned[...] = mine
    strain = [turned[pl.ds(r, 8, stride=16), :] for r in range(9)]
    motion = [turned[pl.ds(9 + r, 8, stride=16), :] for r in range(3)]
    seen = [results[q * 8 : q * 8 + 8, :] for q in range(12)]
    form = [[strain[k * 3 + l] + (1.0 if k == l else 0.0) for l in range(3)] for k in range(3)]
    moved = [
        [
            form[k][l]
            + TIME_STEP * (seen[k * 4 + 1] * form[0][l] + seen[k * 4 + 2] * form[1][l] + seen[k * 4 + 3] * form[2][l])
            for l in range(3)
        ]
        for k in range(3)
    ]
    for k in range(3):
        for l in range(3):
            reply_turned[pl.ds(k * 3 + l, 8, stride=16), :] = moved[k][l]
    reply[...] = reply_turned[...].T.reshape(16, 8, 128)
    third = over_solid(reply, reply_middle, send_c, recv_c, own_sem.at[2])
    start(third)

    stress = {}
    for k in range(3):
        for m in range(k, 3):
            value = moved[k][0] * moved[m][0] + moved[k][1] * moved[m][1] + moved[k][2] * moved[m][2]
            stress[k, m] = stress[m, k] = value - 1.0 if k == m else value
    drag = [SPRING_RATE * (motion[k] - seen[k * 4]) for k in range(3)]
    for pair in range(4):
        lanes = slice(pair * 256, pair * 256 + 256)

        def row(x):
            return jnp.concatenate([x[2 * pair : 2 * pair + 1], x[2 * pair + 1 : 2 * pair + 2]], axis=1)

        for k in range(3):
            node_force = row(drag[k]) * shapes[0, :, lanes]
            for j in range(3):
                node_force = node_force - row(stress[k, j]) * shapes[1 + j, :, lanes]
            high, low = split(node_force)
            nodal[k * 64 : k * 64 + 64, lanes] = high
            nodal[192 + k * 64 : 192 + k * 64 + 64, lanes] = low

    arrive(third)
    fourth = over_dy(reply_middle, reply_arrived, send_d, recv_d, own_sem.at[3])
    start(fourth)

    force = dot_nt(nodal[...], onehot[...])
    for copy in halo:
        copy.wait_recv()
    flipped = left_operand(jnp.concatenate([offsets[w].T for w in range(8)], axis=0))
    edge_lane = iota((32, 512), 1)
    edge_line = iota((32, 512), 0)
    edge_place = jnp.where(
        (edge_lane == (edge_line & 7) * 128 + jnp.where((edge_line & 8) == 0, 0, 127)) & ((edge_line & 7) < 4), 1.0, 0.0
    ).astype(BF16)
    below = jnp.where(me_s > 0, low_z[...], 0.0)
    above = jnp.where(me_s < N_SOLID - 1, high_z[...], 0.0)
    edge_high, edge_low = split(jnp.concatenate([below, above], axis=0).T)
    beside = dot(jnp.concatenate([edge_high, edge_low], axis=1), edge_place)
    lane = iota((64, 512), 1) & 127
    place_z = iota((64, 512), 0) & 3
    half_row = iota((4, 8, 512), 1)
    for k in range(3):
        own = field[k]
        flat = own.reshape(64, 512)
        outer = beside[k * 64 : k * 64 + 64]
        previous = jnp.concatenate([pltpu.roll(flat[:, y * 128 : y * 128 + 128], 1, 1) for y in range(4)], axis=1)
        following = jnp.concatenate([pltpu.roll(flat[:, y * 128 : y * 128 + 128], 127, 1) for y in range(4)], axis=1)
        previous = jnp.where(lane == 0, outer, previous)
        following = jnp.where(lane == 127, outer, following)
        near = jnp.where(place_z == 0, pltpu.roll(previous, 61, 0), 0.0)
        near = near + jnp.where(place_z == 3, pltpu.roll(following, 3, 0), 0.0)
        near = near.reshape(4, 16, 512)
        lower = jnp.concatenate([jnp.where(me_y > 0, low_y[k], 0.0), own[:, 8:16, :384]], axis=2)
        upper = jnp.concatenate([own[:, 0:8, 128:], jnp.where(me_y < N_DY - 1, high_y[k], 0.0)], axis=2)
        lower = jnp.where(half_row < 4, pltpu.roll(lower, 4, 1), 0.0)
        upper = jnp.where(half_row >= 4, pltpu.roll(upper, 4, 1), 0.0)
        near = near + jnp.concatenate([lower, upper], axis=1)
        lower = jnp.where(me_x > 0, low_x[k], 0.0)[None]
        upper = jnp.where(me_x < N_DX - 1, high_x[k], 0.0)[None]
        near = near + jnp.concatenate([lower, jnp.zeros((2, 16, 512), F32), upper], axis=0)
        total = (applied[k] - PENALTY * near).reshape(64, 512)
        total = total - force[k * 64 : k * 64 + 64] - force[192 + k * 64 : 192 + k * 64 + 64]
        result = constrain(total, flipped, config_row)
        for y in range(4):
            fluid[pl.ds(k * 256 + y, 64, stride=4), :] = result[:, y * 128 : y * 128 + 128]
    fluid_out = pltpu.make_async_copy(fluid, fluid_hbm, out_sem.at[0])
    fluid_out.start()

    device_slot = jnp.where((iota((256, 1024), 1) >> 3) == (iota((256, 1024), 0) & 127), 1.0, 0.0).astype(BF16)
    arrive(fourth)
    back_high, back_low = split(reply_arrived[...].reshape(128, 128).T)
    wide = dot(jnp.concatenate([back_high, back_low], axis=1), device_slot)
    slots = jnp.zeros((16, 1024), F32)
    for c in range(8):
        slots = slots + jnp.where(slot_place == c, wide[c * 16 : c * 16 + 16], 0.0)
    for g in range(8):
        deform[pl.ds(g, 16, stride=8), :] = slots[:, g * 128 : g * 128 + 128]
    deform_out = pltpu.make_async_copy(deform.at[0:72], deform_hbm, out_sem.at[1])
    deform_out.start()
    for copies in (first, second, third, fourth):
        for copy in copies[1:]:
            copy.wait_send()
    for copy in halo:
        copy.wait_send()
    fluid_out.wait()
    deform_out.wait()


def shards(velocity, viscosity, cell_config, constraint_offsets, slot_cells, point_coords, strain_offsets, solid_velocity):
    anywhere = pl.BlockSpec(memory_space=pl.ANY)
    vmem = pltpu.VMEM
    dma = pltpu.SemaphoreType.DMA
    fluid, deform = pl.pallas_call(
        kernel,
        out_shape=(jax.ShapeDtypeStruct((768, 128), F32), jax.ShapeDtypeStruct((72, 128), F32)),
        in_specs=[anywhere] * 8,
        out_specs=(anywhere, anywhere),
        scratch_shapes=[
            vmem((768, 128), F32),
            vmem((4, 128), F32),
            vmem((4, 128), jnp.int32),
            vmem((8, 64, 64), F32),
            vmem((8, 128), jnp.int32),
            vmem((128, 128), F32),
            vmem((3, 4, 16, 512), F32),
            vmem((384, 512), BF16),
            vmem((3, 4, 16, 512), F32),
            vmem((512, 1024), BF16),
            vmem((4, 64, 1024), F32),
            vmem((384, 1024), BF16),
            vmem((96, 128), F32),
            vmem((128, 128), F32),
            vmem((16, 8, 128), F32),
            vmem((16, 8, 128), F32),
            vmem((16, 8, 128), F32),
            vmem((16, 8, 128), F32),
            vmem((16, 8, 128), F32),
            vmem((16, 8, 128), F32),
            vmem((128, 128), F32),
            vmem((2, 8, 192), F32),
            vmem((3, 16, 512), F32),
            vmem((3, 16, 512), F32),
            vmem((3, 4, 8, 128), F32),
            vmem((3, 4, 8, 128), F32),
            vmem((8, 192), F32),
            vmem((8, 192), F32),
            vmem((768, 128), F32),
            vmem((128, 128), F32),
            dma((8,)),
            dma((4,)),
            dma((2,)),
            dma((N_SOLID - 1,)),
            dma((N_SOLID - 1,)),
            dma((N_DY - 1,)),
            dma((N_DY - 1,)),
            dma((N_SOLID - 1,)),
            dma((N_SOLID - 1,)),
            dma((N_DY - 1,)),
            dma((N_DY - 1,)),
            dma((6,)),
            dma((6,)),
        ],
        compiler_params=pltpu.CompilerParams(collective_id=0, has_side_effects=True),
    )(
        velocity.reshape(768, 128),
        viscosity.reshape(4, 128),
        cell_config.reshape(4, 128),
        constraint_offsets,
        slot_cells.reshape(8, 128),
        point_coords.reshape(24, 128),
        strain_offsets.reshape(72, 128),
        solid_velocity.reshape(24, 128),
    )
    return fluid.reshape(velocity.shape), deform.reshape(strain_offsets.shape)


def solution(mesh):
    return jax.shard_map(
        shards,
        mesh=mesh,
        in_specs=(
            P(None, None, None, None, "dx", "dy", "solid"),
            P("dx", "dy", "solid"),
            P("dx", "dy", "solid"),
            P(),
            P("dx", ("dy", "solid"), None),
            P(None, "dx", ("dy", "solid"), None),
            P(None, None, "dx", ("dy", "solid"), None),
            P(None, "dx", ("dy", "solid"), None),
        ),
        out_specs=(
            P(None, None, None, None, "dx", "dy", "solid"),
            P(None, None, "dx", ("dy", "solid"), None),
        ),
        check_vma=False,
    )
```

```python
import jax
import jax.numpy as jnp
from jax import lax
from jax.experimental import pallas as pl
from jax.experimental.pallas import tpu as pltpu
from jax.sharding import PartitionSpec as P

F32 = jnp.float32
BF16 = jnp.bfloat16
TIME_STEP = 0.05
SPRING_RATE = 2.0
PENALTY = 4.0
NODE_POINTS = (0.0, 1.0 / 3.0, 2.0 / 3.0, 1.0)
N_DX, N_DY, N_SOLID = 4, 16, 8
MESH = pl.DeviceIdType.MESH


def iota(shape, dim):
    return lax.broadcasted_iota(jnp.int32, shape, dim)


def split(x):
    high = x.astype(BF16)
    return high, (x - high.astype(F32)).astype(BF16)


def dot(a, b):
    return lax.dot_general(a, b, (((1,), (0,)), ((), ())), preferred_element_type=F32)


def dot_nt(a, b):
    return lax.dot_general(a, b, (((1,), (1,)), ((), ())), preferred_element_type=F32)


def lagrange(coord):
    values = []
    slopes = []
    for which in range(4):
        others = [NODE_POINTS[j] for j in range(4) if j != which]
        denom = 1.0
        for other in others:
            denom = denom * (NODE_POINTS[which] - other)
        first = coord - others[0]
        second = coord - others[1]
        third = coord - others[2]
        scale = 1.0 / denom
        values.append(first * second * third * scale)
        slopes.append((second * third + first * third + first * second) * scale)
    return values, slopes


def pick(rows, index):
    out = jnp.where(index == 0, rows[0], rows[1])
    return jnp.where(index < 2, out, jnp.where(index == 2, rows[2], rows[3]))


def deformed(strain, grad):
    form = [[strain[k * 3 + l] + (1.0 if k == l else 0.0) for l in range(3)] for k in range(3)]
    return [
        [
            form[k][l]
            + TIME_STEP * (grad[k * 3] * form[0][l] + grad[k * 3 + 1] * form[1][l] + grad[k * 3 + 2] * form[2][l])
            for l in range(3)
        ]
        for k in range(3)
    ]


def stiffness():
    row, col = iota((64, 64), 0), iota((64, 64), 1)
    total = jnp.where(row == col, 6.0, 0.0)
    for step in (16, 4, 1):
        place_row, place_col = (row // step) % 4, (col // step) % 4
        same = (row - place_row * step) == (col - place_col * step)
        near = jnp.abs(place_row - place_col) == 1
        total = total - jnp.where(same & near, 1.0, 0.0)
    return total


def left_operand(stack):
    high, low = split(stack)
    return jnp.concatenate([high, high, low], axis=1)


def constrain(field, left, config):
    high, low = split(field)
    product = dot(left, jnp.concatenate([high, low, high], axis=0))
    total = field
    for which in range(8):
        total = total + jnp.where(config == which, product[which * 64 : which * 64 + 64], 0.0)
    return total


def kernel(
    vel_hbm, visc_hbm, config_hbm, offsets_hbm, cells_hbm, coords_hbm, strain_hbm, motion_hbm,
    fluid, deform,
    vel, visc, config, offsets, cells, items,
    field, halves, applied, onehot, shapes, nodal, results, turned, grads,
    packet, middle, arrived, reply, reply_middle, reply_arrived, reply_turned,
    edge, low_x, high_x, low_y, high_y, low_z, high_z,
    in_sem, own_sem,
    send_a, recv_a, send_b, recv_b, send_c, recv_c, send_d, recv_d, send_h, recv_h,
):
    me_x, me_y, me_s = lax.axis_index("dx"), lax.axis_index("dy"), lax.axis_index("solid")

    barrier = pltpu.get_barrier_semaphore()
    for step in range(1, N_SOLID):
        pl.semaphore_signal(barrier, inc=1, device_id={"solid": lax.rem(me_s + step, N_SOLID)}, device_id_type=MESH)
    for step in range(1, N_DY):
        pl.semaphore_signal(barrier, inc=1, device_id={"dy": lax.rem(me_y + step, N_DY)}, device_id_type=MESH)
    for step in (1, N_DX - 1):
        pl.semaphore_signal(barrier, inc=1, device_id={"dx": lax.rem(me_x + step, N_DX)}, device_id_type=MESH)

    loads = [
        pltpu.make_async_copy(source, target, in_sem.at[which])
        for which, (source, target) in enumerate(
            (
                (strain_hbm, items.at[0:72]),
                (motion_hbm, items.at[72:96]),
                (coords_hbm, items.at[96:120]),
                (cells_hbm, cells),
                (vel_hbm, vel),
                (offsets_hbm, offsets),
                (config_hbm, config),
                (visc_hbm, visc),
            )
        )
    ]
    for load in loads:
        load.start()

    def over_solid(source, target, send, recv, own):
        copies = [pltpu.make_async_copy(source.at[:, me_s], target.at[:, me_s], own)]
        for step in range(1, N_SOLID):
            peer = lax.rem(me_s + step, N_SOLID)
            copies.append(
                pltpu.make_async_remote_copy(
                    src_ref=source.at[:, peer],
                    dst_ref=target.at[:, me_s],
                    send_sem=send.at[step - 1],
                    recv_sem=recv.at[step - 1],
                    device_id={"solid": peer},
                    device_id_type=MESH,
                )
            )
        return copies

    def over_dy(source, target, send, recv, own):
        copies = [pltpu.make_async_copy(source.at[me_y], target.at[me_y], own)]
        for step in range(1, N_DY):
            peer = lax.rem(me_y + step, N_DY)
            copies.append(
                pltpu.make_async_remote_copy(
                    src_ref=source.at[peer],
                    dst_ref=target.at[me_y],
                    send_sem=send.at[step - 1],
                    recv_sem=recv.at[step - 1],
                    device_id={"dy": peer},
                    device_id_type=MESH,
                )
            )
        return copies

    def start(copies):
        for copy in copies:
            copy.start()

    def arrive(copies):
        copies[0].wait()
        for copy in copies[1:]:
            copy.wait_recv()

    slot_place = iota((1, 1024), 1) & 7
    for load in loads[:4]:
        load.wait()
    items[120:128, :] = cells[...].astype(F32)
    rows = jnp.concatenate([items[pl.ds(g, 16, stride=8), :] for g in range(8)], axis=1)
    spread = jnp.concatenate([jnp.where(slot_place == c, rows, 0.0) for c in range(8)], axis=0)
    spread_high, spread_low = split(spread)
    slot_device = jnp.where((iota((1024, 128), 0) >> 3) == iota((1024, 128), 1), 1.0, 0.0).astype(BF16)
    packed = dot(spread_high, slot_device) + dot(spread_low, slot_device)
    packet[...] = packed.T.reshape(16, 8, 128)
    turned[...] = packed
    reply_turned[...] = jnp.zeros_like(reply_turned)

    pl.semaphore_wait(barrier, N_SOLID - 1 + N_DY - 1 + 2)
    first = over_dy(packet, middle, send_a, recv_a, own_sem.at[0])
    start(first)

    for load in loads[4:]:
        load.wait()
    own_config = config[...]
    config_row = jnp.concatenate([own_config[y : y + 1] for y in range(4)], axis=1)
    left = left_operand(offsets[...].reshape(512, 64))
    for k in range(3):
        start_field = jnp.concatenate([vel[pl.ds(k * 256 + y, 64, stride=4), :] for y in range(4)], axis=1)
        own = constrain(start_field, left, config_row)
        field[k] = own.reshape(4, 16, 512)
        high, low = split(own)
        halves[k * 64 : k * 64 + 64] = high
        halves[192 + k * 64 : 192 + k * 64 + 64] = low

    points = [turned[pl.ds(12 + j, 8, stride=16), :] for j in range(3)]
    target = turned[pl.ds(15, 8, stride=16), :]
    polys = [lagrange(point) for point in points]
    cell_index = iota((512, 256), 0).astype(F32)
    node_row = iota((16, 256), 0)
    for pair in range(4):
        lanes = slice(pair * 256, pair * 256 + 256)

        def row(x):
            return jnp.concatenate([x[2 * pair : 2 * pair + 1], x[2 * pair + 1 : 2 * pair + 2]], axis=1)

        onehot[:, lanes] = jnp.where(cell_index == row(target), 1.0, 0.0).astype(BF16)
        value_x, slope_x = [[row(x) for x in part] for part in polys[0]]
        value_y, slope_y = [pick([row(x) for x in part], node_row >> 2) for part in polys[1]]
        value_z, slope_z = [pick([row(x) for x in part], node_row & 3) for part in polys[2]]
        plain, along_y, along_z = value_y * value_z, slope_y * value_z, value_y * slope_z
        for a in range(4):
            at = slice(a * 16, a * 16 + 16)
            shapes[0, at, lanes] = value_x[a] * plain
            shapes[1, at, lanes] = slope_x[a] * plain
            shapes[2, at, lanes] = value_x[a] * along_y
            shapes[3, at, lanes] = value_x[a] * along_z
        gathered = dot(halves[...], onehot[:, lanes])
        for k in range(3):
            nodes = gathered[k * 64 : k * 64 + 64] + gathered[192 + k * 64 : 192 + k * 64 + 64]
            for j in range(4):
                total = jnp.sum(nodes * shapes[j, :, lanes], axis=0, keepdims=True)
                line = (k * 4 + j) * 8 + 2 * pair
                results[line : line + 1, :] = total[:, :128]
                results[line + 1 : line + 2, :] = total[:, 128:]
    seen = [results[q * 8 : q * 8 + 8, :] for q in range(12)]
    for k in range(3):
        for j in range(3):
            reply_turned[pl.ds(k * 3 + j, 8, stride=16), :] = seen[k * 4 + 1 + j]
    reply[...] = reply_turned[...].T.reshape(16, 8, 128)
    second = over_dy(reply, reply_middle, send_c, recv_c, own_sem.at[2])
    start(second)

    def remote(source, target, which, where):
        return pltpu.make_async_remote_copy(
            src_ref=source, dst_ref=target, send_sem=send_h.at[which], recv_sem=recv_h.at[which],
            device_id=where, device_id_type=MESH,
        )

    up_x, down_x = lax.rem(me_x + 1, N_DX), lax.rem(me_x + N_DX - 1, N_DX)
    up_y, down_y = lax.rem(me_y + 1, N_DY), lax.rem(me_y + N_DY - 1, N_DY)
    up_s, down_s = lax.rem(me_s + 1, N_SOLID), lax.rem(me_s + N_SOLID - 1, N_SOLID)
    halo = [
        remote(field.at[:, 3], low_x, 0, {"dx": up_x}),
        remote(field.at[:, 0], high_x, 1, {"dx": down_x}),
        remote(field.at[:, :, 8:16, 384:512], low_y, 2, {"dy": up_y}),
        remote(field.at[:, :, 0:8, 0:128], high_y, 3, {"dy": down_y}),
        remote(edge.at[0], low_z, 4, {"solid": up_s}),
        remote(edge.at[1], high_z, 5, {"solid": down_s}),
    ]
    edge_row, edge_col = iota((16, 512), 0), iota((16, 512), 1)
    lane_edge = jnp.where(edge_row < 8, 127, 0)
    edge_pick = jnp.where(
        (edge_col == (edge_row & 7) * 128 + lane_edge) & ((edge_row & 7) < 4), 1.0, 0.0
    ).astype(BF16)
    edges = dot_nt(edge_pick, halves[0:192]) + dot_nt(edge_pick, halves[192:384])
    edge[...] = edges.reshape(2, 8, 192)
    start(halo)

    own_visc = visc[...]
    visc_row = jnp.concatenate([own_visc[y : y + 1] for y in range(4)], axis=1)
    stiff = stiffness().astype(BF16)
    stiff = jnp.concatenate([stiff, stiff], axis=1)
    node = iota((64, 512), 0)
    ends = jnp.zeros((64, 512), F32)
    for step in (16, 4, 1):
        place = (node // step) % 4
        ends = ends + jnp.where((place == 0) | (place == 3), PENALTY, 0.0)
    for k in range(3):
        both = jnp.concatenate([halves[k * 64 : k * 64 + 64], halves[192 + k * 64 : 192 + k * 64 + 64]], axis=0)
        own = field[k].reshape(64, 512)
        applied[k] = (own * (1.0 + ends) + visc_row * dot(stiff, both)).reshape(4, 16, 512)

    arrive(first)
    third = over_solid(middle, arrived, send_b, recv_b, own_sem.at[1])
    start(third)
    arrive(second)
    fourth = over_solid(reply_middle, reply_arrived, send_d, recv_d, own_sem.at[3])
    start(fourth)

    for copy in halo:
        copy.wait_recv()
    flipped = left_operand(jnp.concatenate([offsets[w].T for w in range(8)], axis=0))
    edge_lane = iota((32, 512), 1)
    edge_line = iota((32, 512), 0)
    edge_place = jnp.where(
        (edge_lane == (edge_line & 7) * 128 + jnp.where((edge_line & 8) == 0, 0, 127)) & ((edge_line & 7) < 4), 1.0, 0.0
    ).astype(BF16)
    below = jnp.where(me_s > 0, low_z[...], 0.0)
    above = jnp.where(me_s < N_SOLID - 1, high_z[...], 0.0)
    edge_high, edge_low = split(jnp.concatenate([below, above], axis=0).T)
    beside = dot(jnp.concatenate([edge_high, edge_low], axis=1), edge_place)
    lane = iota((64, 512), 1) & 127
    place_z = iota((64, 512), 0) & 3
    half_row = iota((4, 8, 512), 1)
    for k in range(3):
        own = field[k]
        flat = own.reshape(64, 512)
        outer = beside[k * 64 : k * 64 + 64]
        previous = jnp.concatenate([pltpu.roll(flat[:, y * 128 : y * 128 + 128], 1, 1) for y in range(4)], axis=1)
        following = jnp.concatenate([pltpu.roll(flat[:, y * 128 : y * 128 + 128], 127, 1) for y in range(4)], axis=1)
        previous = jnp.where(lane == 0, outer, previous)
        following = jnp.where(lane == 127, outer, following)
        near = jnp.where(place_z == 0, pltpu.roll(previous, 61, 0), 0.0)
        near = near + jnp.where(place_z == 3, pltpu.roll(following, 3, 0), 0.0)
        near = near.reshape(4, 16, 512)
        lower = jnp.concatenate([jnp.where(me_y > 0, low_y[k], 0.0), own[:, 8:16, :384]], axis=2)
        upper = jnp.concatenate([own[:, 0:8, 128:], jnp.where(me_y < N_DY - 1, high_y[k], 0.0)], axis=2)
        lower = jnp.where(half_row < 4, pltpu.roll(lower, 4, 1), 0.0)
        upper = jnp.where(half_row >= 4, pltpu.roll(upper, 4, 1), 0.0)
        near = near + jnp.concatenate([lower, upper], axis=1)
        lower = jnp.where(me_x > 0, low_x[k], 0.0)[None]
        upper = jnp.where(me_x < N_DX - 1, high_x[k], 0.0)[None]
        near = near + jnp.concatenate([lower, jnp.zeros((2, 16, 512), F32), upper], axis=0)
        applied[k] = applied[k] - PENALTY * near
    device_slot = jnp.where((iota((256, 1024), 1) >> 3) == (iota((256, 1024), 0) & 127), 1.0, 0.0).astype(BF16)

    arrive(third)
    turned[...] = arrived[...].reshape(128, 128).T
    moved = deformed(
        [turned[pl.ds(r, 8, stride=16), :] for r in range(9)],
        [seen[k * 4 + 1 + j] for k in range(3) for j in range(3)],
    )
    motion = [turned[pl.ds(9 + r, 8, stride=16), :] for r in range(3)]
    stress = {}
    for k in range(3):
        for m in range(k, 3):
            value = moved[k][0] * moved[m][0] + moved[k][1] * moved[m][1] + moved[k][2] * moved[m][2]
            stress[k, m] = stress[m, k] = value - 1.0 if k == m else value
    drag = [SPRING_RATE * (motion[k] - seen[k * 4]) for k in range(3)]
    for pair in range(4):
        lanes = slice(pair * 256, pair * 256 + 256)

        def row(x):
            return jnp.concatenate([x[2 * pair : 2 * pair + 1], x[2 * pair + 1 : 2 * pair + 2]], axis=1)

        for k in range(3):
            node_force = row(drag[k]) * shapes[0, :, lanes]
            for j in range(3):
                node_force = node_force - row(stress[k, j]) * shapes[1 + j, :, lanes]
            high, low = split(node_force)
            nodal[k * 64 : k * 64 + 64, lanes] = high
            nodal[192 + k * 64 : 192 + k * 64 + 64, lanes] = low
    force = dot_nt(nodal[...], onehot[...])
    for k in range(3):
        total = applied[k].reshape(64, 512)
        total = total - force[k * 64 : k * 64 + 64] - force[192 + k * 64 : 192 + k * 64 + 64]
        result = constrain(total, flipped, config_row)
        for y in range(4):
            fluid[pl.ds(k * 256 + y, 64, stride=4), :] = result[:, y * 128 : y * 128 + 128]

    arrive(fourth)
    back_high, back_low = split(reply_arrived[...].reshape(128, 128).T)
    wide = dot(jnp.concatenate([back_high, back_low], axis=1), device_slot)
    slots = jnp.zeros((16, 1024), F32)
    for c in range(8):
        slots = slots + jnp.where(slot_place == c, wide[c * 16 : c * 16 + 16], 0.0)
    for g in range(8):
        grads[pl.ds(g, 16, stride=8), :] = slots[:, g * 128 : g * 128 + 128]
    moved = deformed(
        [items[r * 8 : r * 8 + 8, :] for r in range(9)],
        [grads[r * 8 : r * 8 + 8, :] for r in range(9)],
    )
    for k in range(3):
        for l in range(3):
            deform[(k * 3 + l) * 8 : (k * 3 + l) * 8 + 8, :] = moved[k][l]
    for copies in (first, second, third, fourth):
        for copy in copies[1:]:
            copy.wait_send()
    for copy in halo:
        copy.wait_send()


def shards(velocity, viscosity, cell_config, constraint_offsets, slot_cells, point_coords, strain_offsets, solid_velocity):
    anywhere = pl.BlockSpec(memory_space=pl.ANY)
    inside = pl.BlockSpec(memory_space=pltpu.VMEM)
    vmem = pltpu.VMEM
    dma = pltpu.SemaphoreType.DMA
    fluid, deform = pl.pallas_call(
        kernel,
        out_shape=(vmem((768, 128), F32), vmem((72, 128), F32)),
        in_specs=[anywhere] * 8,
        out_specs=(inside, inside),
        scratch_shapes=[
            vmem((768, 128), F32),
            vmem((4, 128), F32),
            vmem((4, 128), jnp.int32),
            vmem((8, 64, 64), F32),
            vmem((8, 128), jnp.int32),
            vmem((128, 128), F32),
            vmem((3, 4, 16, 512), F32),
            vmem((384, 512), BF16),
            vmem((3, 4, 16, 512), F32),
            vmem((512, 1024), BF16),
            vmem((4, 64, 1024), F32),
            vmem((384, 1024), BF16),
            vmem((96, 128), F32),
            vmem((128, 128), F32),
            vmem((128, 128), F32),
            vmem((16, 8, 128), F32),
            vmem((16, 8, 128), F32),
            vmem((16, 8, 128), F32),
            vmem((16, 8, 128), F32),
            vmem((16, 8, 128), F32),
            vmem((16, 8, 128), F32),
            vmem((128, 128), F32),
            vmem((2, 8, 192), F32),
            vmem((3, 16, 512), F32),
            vmem((3, 16, 512), F32),
            vmem((3, 4, 8, 128), F32),
            vmem((3, 4, 8, 128), F32),
            vmem((8, 192), F32),
            vmem((8, 192), F32),
            dma((8,)),
            dma((4,)),
            dma((N_DY - 1,)),
            dma((N_DY - 1,)),
            dma((N_SOLID - 1,)),
            dma((N_SOLID - 1,)),
            dma((N_DY - 1,)),
            dma((N_DY - 1,)),
            dma((N_SOLID - 1,)),
            dma((N_SOLID - 1,)),
            dma((6,)),
            dma((6,)),
        ],
        compiler_params=pltpu.CompilerParams(collective_id=0, has_side_effects=True),
    )(
        velocity.reshape(768, 128),
        viscosity.reshape(4, 128),
        cell_config.reshape(4, 128),
        constraint_offsets,
        slot_cells.reshape(8, 128),
        point_coords.reshape(24, 128),
        strain_offsets.reshape(72, 128),
        solid_velocity.reshape(24, 128),
    )
    return fluid.reshape(velocity.shape), deform.reshape(strain_offsets.shape)


def solution(mesh):
    return jax.shard_map(
        shards,
        mesh=mesh,
        in_specs=(
            P(None, None, None, None, "dx", "dy", "solid"),
            P("dx", "dy", "solid"),
            P("dx", "dy", "solid"),
            P(),
            P("dx", ("dy", "solid"), None),
            P(None, "dx", ("dy", "solid"), None),
            P(None, None, "dx", ("dy", "solid"), None),
            P(None, "dx", ("dy", "solid"), None),
        ),
        out_specs=(
            P(None, None, None, None, "dx", "dy", "solid"),
            P(None, None, "dx", ("dy", "solid"), None),
        ),
        check_vma=False,
    )
```

```python
import jax
import jax.numpy as jnp
from jax import lax
from jax.experimental import pallas as pl
from jax.experimental.pallas import tpu as pltpu
from jax.sharding import PartitionSpec as P

F32 = jnp.float32
BF16 = jnp.bfloat16
TIME_STEP = 0.05
SPRING_RATE = 2.0
PENALTY = 4.0
NODE_POINTS = (0.0, 1.0 / 3.0, 2.0 / 3.0, 1.0)
N_DX, N_DY, N_SOLID = 4, 16, 8
MESH = pl.DeviceIdType.MESH


def iota(shape, dim):
    return lax.broadcasted_iota(jnp.int32, shape, dim)


def split(x):
    high = x.astype(BF16)
    return high, (x - high.astype(F32)).astype(BF16)


def dot(a, b):
    return lax.dot_general(a, b, (((1,), (0,)), ((), ())), preferred_element_type=F32)


def dot_nt(a, b):
    return lax.dot_general(a, b, (((1,), (1,)), ((), ())), preferred_element_type=F32)


def lagrange(coord):
    values = []
    slopes = []
    for which in range(4):
        others = [NODE_POINTS[j] for j in range(4) if j != which]
        denom = 1.0
        for other in others:
            denom = denom * (NODE_POINTS[which] - other)
        first = coord - others[0]
        second = coord - others[1]
        third = coord - others[2]
        scale = 1.0 / denom
        values.append(first * second * third * scale)
        slopes.append((second * third + first * third + first * second) * scale)
    return values, slopes


def pick(rows, index):
    out = jnp.where(index == 0, rows[0], rows[1])
    return jnp.where(index < 2, out, jnp.where(index == 2, rows[2], rows[3]))


def deformed(strain, grad):
    form = [[strain[k * 3 + l] + (1.0 if k == l else 0.0) for l in range(3)] for k in range(3)]
    return [
        [
            form[k][l]
            + TIME_STEP * (grad[k * 3] * form[0][l] + grad[k * 3 + 1] * form[1][l] + grad[k * 3 + 2] * form[2][l])
            for l in range(3)
        ]
        for k in range(3)
    ]


def stiffness():
    row, col = iota((64, 64), 0), iota((64, 64), 1)
    total = jnp.where(row == col, 6.0, 0.0)
    for step in (16, 4, 1):
        place_row, place_col = (row // step) % 4, (col // step) % 4
        same = (row - place_row * step) == (col - place_col * step)
        near = jnp.abs(place_row - place_col) == 1
        total = total - jnp.where(same & near, 1.0, 0.0)
    return total


def left_operand(stack):
    high, low = split(stack)
    return jnp.concatenate([high, high, low], axis=1)


def constrain(field, left, config):
    high, low = split(field)
    product = dot(left, jnp.concatenate([high, low, high], axis=0))
    total = field
    for which in range(8):
        total = total + jnp.where(config == which, product[which * 64 : which * 64 + 64], 0.0)
    return total


def kernel(
    vel_hbm, visc_hbm, config_hbm, offsets_hbm, cells_hbm, coords_hbm, strain_hbm, motion_hbm,
    fluid, deform,
    vel, visc, config, offsets, cells, items,
    field, halves, applied, onehot, shapes, nodal, results, turned, grads,
    packet, middle, arrived, reply, reply_middle, reply_arrived, reply_turned,
    edge, low_x, high_x, low_y, high_y, low_z, high_z,
    in_sem, own_sem, entered_y, entered_s,
    send_a, recv_a, send_b, recv_b, send_c, recv_c, send_d, recv_d, send_h, recv_h,
):
    me_x, me_y, me_s = lax.axis_index("dx"), lax.axis_index("dy"), lax.axis_index("solid")

    def rank(place):
        return jnp.where(place < 4, place, 11 - place)

    def later_s(step):
        return rank(lax.rem(me_s + step, N_SOLID)) > rank(me_s)

    barrier = pltpu.get_barrier_semaphore()
    for step in range(1, N_DY):

        @pl.when(me_y + step < N_DY)
        def _():
            pl.semaphore_signal(barrier, inc=1, device_id={"dy": me_y + step}, device_id_type=MESH)

    for step in range(1, N_SOLID):

        @pl.when(later_s(step))
        def _():
            pl.semaphore_signal(barrier, inc=1, device_id={"solid": lax.rem(me_s + step, N_SOLID)}, device_id_type=MESH)

    for step in (1, N_DX - 1):
        pl.semaphore_signal(barrier, inc=1, device_id={"dx": lax.rem(me_x + step, N_DX)}, device_id_type=MESH)

    loads = [
        pltpu.make_async_copy(source, target, in_sem.at[which])
        for which, (source, target) in enumerate(
            (
                (strain_hbm, items.at[0:72]),
                (motion_hbm, items.at[72:96]),
                (coords_hbm, items.at[96:120]),
                (cells_hbm, cells),
                (vel_hbm, vel),
                (offsets_hbm, offsets),
                (config_hbm, config),
                (visc_hbm, visc),
            )
        )
    ]
    for load in loads:
        load.start()

    def over_solid(source, target, send, recv, own):
        copies = [pltpu.make_async_copy(source.at[:, me_s], target.at[:, me_s], own)]
        for step in range(1, N_SOLID):
            peer = lax.rem(me_s + step, N_SOLID)
            copies.append(
                pltpu.make_async_remote_copy(
                    src_ref=source.at[:, peer],
                    dst_ref=target.at[:, me_s],
                    send_sem=send.at[step - 1],
                    recv_sem=recv.at[step - 1],
                    device_id={"solid": peer},
                    device_id_type=MESH,
                )
            )
        return copies

    def over_dy(source, target, send, recv, own):
        copies = [pltpu.make_async_copy(source.at[me_y], target.at[me_y], own)]
        for step in range(1, N_DY):
            peer = lax.rem(me_y + step, N_DY)
            copies.append(
                pltpu.make_async_remote_copy(
                    src_ref=source.at[peer],
                    dst_ref=target.at[me_y],
                    send_sem=send.at[step - 1],
                    recv_sem=recv.at[step - 1],
                    device_id={"dy": peer},
                    device_id_type=MESH,
                )
            )
        return copies

    def start(copies):
        for copy in copies:
            copy.start()

    def start_early(copies):
        copies[0].start()
        for step in range(1, N_DY):

            @pl.when(me_y + step >= N_DY)
            def _():
                copies[step].start()

    def start_late(groups):
        for step in range(1, N_DY):

            @pl.when(me_y + step < N_DY)
            def _():
                pl.semaphore_wait(entered_y.at[step - 1], 1)
                for copies in groups:
                    copies[step].start()

    def greet_s():
        for step in range(1, N_SOLID):

            @pl.when(later_s(step))
            def _():
                pl.semaphore_wait(entered_s.at[step - 1], 1)

    def arrive(copies):
        copies[0].wait()
        for copy in copies[1:]:
            copy.wait_recv()

    slot_place = iota((1, 1024), 1) & 7
    for load in loads[:4]:
        load.wait()
    items[120:128, :] = cells[...].astype(F32)
    rows = jnp.concatenate([items[pl.ds(g, 16, stride=8), :] for g in range(8)], axis=1)
    spread = jnp.concatenate([jnp.where(slot_place == c, rows, 0.0) for c in range(8)], axis=0)
    spread_high, spread_low = split(spread)
    slot_device = jnp.where((iota((1024, 128), 0) >> 3) == iota((1024, 128), 1), 1.0, 0.0).astype(BF16)
    packed = dot(spread_high, slot_device) + dot(spread_low, slot_device)
    packet[...] = packed.T.reshape(16, 8, 128)
    turned[...] = packed
    reply_turned[...] = jnp.zeros_like(reply_turned)

    pl.semaphore_wait(barrier, me_y + rank(me_s) + 2)
    for step in range(1, N_DY):

        @pl.when(me_y >= step)
        def _():
            pl.semaphore_signal(entered_y.at[step - 1], inc=1, device_id={"dy": me_y - step}, device_id_type=MESH)

    for step in range(1, N_SOLID):

        @pl.when(jnp.logical_not(later_s(step)))
        def _():
            pl.semaphore_signal(
                entered_s.at[N_SOLID - 1 - step],
                inc=1,
                device_id={"solid": lax.rem(me_s + step, N_SOLID)},
                device_id_type=MESH,
            )

    first = over_dy(packet, middle, send_a, recv_a, own_sem.at[0])
    start_early(first)

    for load in loads[4:]:
        load.wait()
    own_config = config[...]
    config_row = jnp.concatenate([own_config[y : y + 1] for y in range(4)], axis=1)
    left = left_operand(offsets[...].reshape(512, 64))
    for k in range(3):
        start_field = jnp.concatenate([vel[pl.ds(k * 256 + y, 64, stride=4), :] for y in range(4)], axis=1)
        own = constrain(start_field, left, config_row)
        field[k] = own.reshape(4, 16, 512)
        high, low = split(own)
        halves[k * 64 : k * 64 + 64] = high
        halves[192 + k * 64 : 192 + k * 64 + 64] = low

    points = [turned[pl.ds(12 + j, 8, stride=16), :] for j in range(3)]
    target = turned[pl.ds(15, 8, stride=16), :]
    polys = [lagrange(point) for point in points]
    cell_index = iota((512, 256), 0).astype(F32)
    node_row = iota((16, 256), 0)
    for pair in range(4):
        lanes = slice(pair * 256, pair * 256 + 256)

        def row(x):
            return jnp.concatenate([x[2 * pair : 2 * pair + 1], x[2 * pair + 1 : 2 * pair + 2]], axis=1)

        onehot[:, lanes] = jnp.where(cell_index == row(target), 1.0, 0.0).astype(BF16)
        value_x, slope_x = [[row(x) for x in part] for part in polys[0]]
        value_y, slope_y = [pick([row(x) for x in part], node_row >> 2) for part in polys[1]]
        value_z, slope_z = [pick([row(x) for x in part], node_row & 3) for part in polys[2]]
        plain, along_y, along_z = value_y * value_z, slope_y * value_z, value_y * slope_z
        for a in range(4):
            at = slice(a * 16, a * 16 + 16)
            shapes[0, at, lanes] = value_x[a] * plain
            shapes[1, at, lanes] = slope_x[a] * plain
            shapes[2, at, lanes] = value_x[a] * along_y
            shapes[3, at, lanes] = value_x[a] * along_z
        gathered = dot(halves[...], onehot[:, lanes])
        for k in range(3):
            nodes = gathered[k * 64 : k * 64 + 64] + gathered[192 + k * 64 : 192 + k * 64 + 64]
            for j in range(4):
                total = jnp.sum(nodes * shapes[j, :, lanes], axis=0, keepdims=True)
                line = (k * 4 + j) * 8 + 2 * pair
                results[line : line + 1, :] = total[:, :128]
                results[line + 1 : line + 2, :] = total[:, 128:]
    seen = [results[q * 8 : q * 8 + 8, :] for q in range(12)]
    for k in range(3):
        for j in range(3):
            reply_turned[pl.ds(k * 3 + j, 8, stride=16), :] = seen[k * 4 + 1 + j]
    reply[...] = reply_turned[...].T.reshape(16, 8, 128)
    second = over_dy(reply, reply_middle, send_c, recv_c, own_sem.at[2])
    start_early(second)
    start_late([first, second])


    def remote(source, target, which, where):
        return pltpu.make_async_remote_copy(
            src_ref=source, dst_ref=target, send_sem=send_h.at[which], recv_sem=recv_h.at[which],
            device_id=where, device_id_type=MESH,
        )

    up_x, down_x = lax.rem(me_x + 1, N_DX), lax.rem(me_x + N_DX - 1, N_DX)
    up_y, down_y = lax.rem(me_y + 1, N_DY), lax.rem(me_y + N_DY - 1, N_DY)
    up_s, down_s = lax.rem(me_s + 1, N_SOLID), lax.rem(me_s + N_SOLID - 1, N_SOLID)
    halo = [
        remote(field.at[:, 3], low_x, 0, {"dx": up_x}),
        remote(field.at[:, 0], high_x, 1, {"dx": down_x}),
        remote(field.at[:, :, 8:16, 384:512], low_y, 2, {"dy": up_y}),
        remote(field.at[:, :, 0:8, 0:128], high_y, 3, {"dy": down_y}),
        remote(edge.at[0], low_z, 4, {"solid": up_s}),
        remote(edge.at[1], high_z, 5, {"solid": down_s}),
    ]
    start(halo[:4])
    greet_s()
    edge_row, edge_col = iota((16, 512), 0), iota((16, 512), 1)
    lane_edge = jnp.where(edge_row < 8, 127, 0)
    edge_pick = jnp.where(
        (edge_col == (edge_row & 7) * 128 + lane_edge) & ((edge_row & 7) < 4), 1.0, 0.0
    ).astype(BF16)
    edges = dot_nt(edge_pick, halves[0:192]) + dot_nt(edge_pick, halves[192:384])
    edge[...] = edges.reshape(2, 8, 192)
    start(halo[4:])

    own_visc = visc[...]
    visc_row = jnp.concatenate([own_visc[y : y + 1] for y in range(4)], axis=1)
    stiff = stiffness().astype(BF16)
    stiff = jnp.concatenate([stiff, stiff], axis=1)
    node = iota((64, 512), 0)
    ends = jnp.zeros((64, 512), F32)
    for step in (16, 4, 1):
        place = (node // step) % 4
        ends = ends + jnp.where((place == 0) | (place == 3), PENALTY, 0.0)
    for k in range(3):
        both = jnp.concatenate([halves[k * 64 : k * 64 + 64], halves[192 + k * 64 : 192 + k * 64 + 64]], axis=0)
        own = field[k].reshape(64, 512)
        applied[k] = (own * (1.0 + ends) + visc_row * dot(stiff, both)).reshape(4, 16, 512)

    arrive(first)
    third = over_solid(middle, arrived, send_b, recv_b, own_sem.at[1])
    start(third)
    arrive(second)
    fourth = over_solid(reply_middle, reply_arrived, send_d, recv_d, own_sem.at[3])
    start(fourth)

    for copy in halo:
        copy.wait_recv()
    flipped = left_operand(jnp.concatenate([offsets[w].T for w in range(8)], axis=0))
    edge_lane = iota((32, 512), 1)
    edge_line = iota((32, 512), 0)
    edge_place = jnp.where(
        (edge_lane == (edge_line & 7) * 128 + jnp.where((edge_line & 8) == 0, 0, 127)) & ((edge_line & 7) < 4), 1.0, 0.0
    ).astype(BF16)
    below = jnp.where(me_s > 0, low_z[...], 0.0)
    above = jnp.where(me_s < N_SOLID - 1, high_z[...], 0.0)
    edge_high, edge_low = split(jnp.concatenate([below, above], axis=0).T)
    beside = dot(jnp.concatenate([edge_high, edge_low], axis=1), edge_place)
    lane = iota((64, 512), 1) & 127
    place_z = iota((64, 512), 0) & 3
    half_row = iota((4, 8, 512), 1)
    for k in range(3):
        own = field[k]
        flat = own.reshape(64, 512)
        outer = beside[k * 64 : k * 64 + 64]
        previous = jnp.concatenate([pltpu.roll(flat[:, y * 128 : y * 128 + 128], 1, 1) for y in range(4)], axis=1)
        following = jnp.concatenate([pltpu.roll(flat[:, y * 128 : y * 128 + 128], 127, 1) for y in range(4)], axis=1)
        previous = jnp.where(lane == 0, outer, previous)
        following = jnp.where(lane == 127, outer, following)
        near = jnp.where(place_z == 0, pltpu.roll(previous, 61, 0), 0.0)
        near = near + jnp.where(place_z == 3, pltpu.roll(following, 3, 0), 0.0)
        near = near.reshape(4, 16, 512)
        lower = jnp.concatenate([jnp.where(me_y > 0, low_y[k], 0.0), own[:, 8:16, :384]], axis=2)
        upper = jnp.concatenate([own[:, 0:8, 128:], jnp.where(me_y < N_DY - 1, high_y[k], 0.0)], axis=2)
        lower = jnp.where(half_row < 4, pltpu.roll(lower, 4, 1), 0.0)
        upper = jnp.where(half_row >= 4, pltpu.roll(upper, 4, 1), 0.0)
        near = near + jnp.concatenate([lower, upper], axis=1)
        lower = jnp.where(me_x > 0, low_x[k], 0.0)[None]
        upper = jnp.where(me_x < N_DX - 1, high_x[k], 0.0)[None]
        near = near + jnp.concatenate([lower, jnp.zeros((2, 16, 512), F32), upper], axis=0)
        applied[k] = applied[k] - PENALTY * near
    device_slot = jnp.where((iota((256, 1024), 1) >> 3) == (iota((256, 1024), 0) & 127), 1.0, 0.0).astype(BF16)

    arrive(third)
    turned[...] = arrived[...].reshape(128, 128).T
    moved = deformed(
        [turned[pl.ds(r, 8, stride=16), :] for r in range(9)],
        [seen[k * 4 + 1 + j] for k in range(3) for j in range(3)],
    )
    motion = [turned[pl.ds(9 + r, 8, stride=16), :] for r in range(3)]
    stress = {}
    for k in range(3):
        for m in range(k, 3):
            value = moved[k][0] * moved[m][0] + moved[k][1] * moved[m][1] + moved[k][2] * moved[m][2]
            stress[k, m] = stress[m, k] = value - 1.0 if k == m else value
    drag = [SPRING_RATE * (motion[k] - seen[k * 4]) for k in range(3)]
    for pair in range(4):
        lanes = slice(pair * 256, pair * 256 + 256)

        def row(x):
            return jnp.concatenate([x[2 * pair : 2 * pair + 1], x[2 * pair + 1 : 2 * pair + 2]], axis=1)

        for k in range(3):
            node_force = row(drag[k]) * shapes[0, :, lanes]
            for j in range(3):
                node_force = node_force - row(stress[k, j]) * shapes[1 + j, :, lanes]
            high, low = split(node_force)
            nodal[k * 64 : k * 64 + 64, lanes] = high
            nodal[192 + k * 64 : 192 + k * 64 + 64, lanes] = low
    force = dot_nt(nodal[...], onehot[...])
    for k in range(3):
        total = applied[k].reshape(64, 512)
        total = total - force[k * 64 : k * 64 + 64] - force[192 + k * 64 : 192 + k * 64 + 64]
        result = constrain(total, flipped, config_row)
        for y in range(4):
            fluid[pl.ds(k * 256 + y, 64, stride=4), :] = result[:, y * 128 : y * 128 + 128]

    arrive(fourth)
    back_high, back_low = split(reply_arrived[...].reshape(128, 128).T)
    wide = dot(jnp.concatenate([back_high, back_low], axis=1), device_slot)
    slots = jnp.zeros((16, 1024), F32)
    for c in range(8):
        slots = slots + jnp.where(slot_place == c, wide[c * 16 : c * 16 + 16], 0.0)
    for g in range(8):
        grads[pl.ds(g, 16, stride=8), :] = slots[:, g * 128 : g * 128 + 128]
    moved = deformed(
        [items[r * 8 : r * 8 + 8, :] for r in range(9)],
        [grads[r * 8 : r * 8 + 8, :] for r in range(9)],
    )
    for k in range(3):
        for l in range(3):
            deform[(k * 3 + l) * 8 : (k * 3 + l) * 8 + 8, :] = moved[k][l]
    for copies in (first, second, third, fourth):
        for copy in copies[1:]:
            copy.wait_send()
    for copy in halo:
        copy.wait_send()


def place_kernel(fluid, deform, fluid_hbm, deform_hbm, sem):
    copies = [
        pltpu.make_async_copy(fluid, fluid_hbm, sem.at[0]),
        pltpu.make_async_copy(deform, deform_hbm, sem.at[1]),
    ]
    for copy in copies:
        copy.start()
    for copy in copies:
        copy.wait()


def shards(velocity, viscosity, cell_config, constraint_offsets, slot_cells, point_coords, strain_offsets, solid_velocity):
    anywhere = pl.BlockSpec(memory_space=pl.ANY)
    inside = pl.BlockSpec(memory_space=pltpu.VMEM)
    vmem = pltpu.VMEM
    dma = pltpu.SemaphoreType.DMA
    fluid, deform = pl.pallas_call(
        kernel,
        out_shape=(vmem((768, 128), F32), vmem((72, 128), F32)),
        in_specs=[anywhere] * 8,
        out_specs=(inside, inside),
        scratch_shapes=[
            vmem((768, 128), F32),
            vmem((4, 128), F32),
            vmem((4, 128), jnp.int32),
            vmem((8, 64, 64), F32),
            vmem((8, 128), jnp.int32),
            vmem((128, 128), F32),
            vmem((3, 4, 16, 512), F32),
            vmem((384, 512), BF16),
            vmem((3, 4, 16, 512), F32),
            vmem((512, 1024), BF16),
            vmem((4, 64, 1024), F32),
            vmem((384, 1024), BF16),
            vmem((96, 128), F32),
            vmem((128, 128), F32),
            vmem((128, 128), F32),
            vmem((16, 8, 128), F32),
            vmem((16, 8, 128), F32),
            vmem((16, 8, 128), F32),
            vmem((16, 8, 128), F32),
            vmem((16, 8, 128), F32),
            vmem((16, 8, 128), F32),
            vmem((128, 128), F32),
            vmem((2, 8, 192), F32),
            vmem((3, 16, 512), F32),
            vmem((3, 16, 512), F32),
            vmem((3, 4, 8, 128), F32),
            vmem((3, 4, 8, 128), F32),
            vmem((8, 192), F32),
            vmem((8, 192), F32),
            dma((8,)),
            dma((4,)),
            pltpu.SemaphoreType.REGULAR((N_DY - 1,)),
            pltpu.SemaphoreType.REGULAR((N_SOLID - 1,)),
            dma((N_DY - 1,)),
            dma((N_DY - 1,)),
            dma((N_SOLID - 1,)),
            dma((N_SOLID - 1,)),
            dma((N_DY - 1,)),
            dma((N_DY - 1,)),
            dma((N_SOLID - 1,)),
            dma((N_SOLID - 1,)),
            dma((6,)),
            dma((6,)),
        ],
        compiler_params=pltpu.CompilerParams(collective_id=0, has_side_effects=True),
    )(
        velocity.reshape(768, 128),
        viscosity.reshape(4, 128),
        cell_config.reshape(4, 128),
        constraint_offsets,
        slot_cells.reshape(8, 128),
        point_coords.reshape(24, 128),
        strain_offsets.reshape(72, 128),
        solid_velocity.reshape(24, 128),
    )
    fluid, deform = pl.pallas_call(
        place_kernel,
        out_shape=(jax.ShapeDtypeStruct((768, 128), F32), jax.ShapeDtypeStruct((72, 128), F32)),
        in_specs=[inside, inside],
        out_specs=(anywhere, anywhere),
        scratch_shapes=[dma((2,))],
    )(pltpu.with_memory_space_constraint(fluid, pltpu.VMEM), pltpu.with_memory_space_constraint(deform, pltpu.VMEM))
    return fluid.reshape(velocity.shape), deform.reshape(strain_offsets.shape)


def solution(mesh):
    return jax.shard_map(
        shards,
        mesh=mesh,
        in_specs=(
            P(None, None, None, None, "dx", "dy", "solid"),
            P("dx", "dy", "solid"),
            P("dx", "dy", "solid"),
            P(),
            P("dx", ("dy", "solid"), None),
            P(None, "dx", ("dy", "solid"), None),
            P(None, None, "dx", ("dy", "solid"), None),
            P(None, "dx", ("dy", "solid"), None),
        ),
        out_specs=(
            P(None, None, None, None, "dx", "dy", "solid"),
            P(None, None, "dx", ("dy", "solid"), None),
        ),
        check_vma=False,
    )
```

```python
import jax
import jax.numpy as jnp
from jax import lax
from jax.experimental import pallas as pl
from jax.experimental.pallas import tpu as pltpu
from jax.sharding import PartitionSpec as P

F32 = jnp.float32
BF16 = jnp.bfloat16
TIME_STEP = 0.05
SPRING_RATE = 2.0
PENALTY = 4.0
NODE_POINTS = (0.0, 1.0 / 3.0, 2.0 / 3.0, 1.0)
N_DX, N_DY, N_SOLID = 4, 16, 8
MESH = pl.DeviceIdType.MESH


def iota(shape, dim):
    return lax.broadcasted_iota(jnp.int32, shape, dim)


def split(x):
    high = x.astype(BF16)
    return high, (x - high.astype(F32)).astype(BF16)


def dot(a, b):
    return lax.dot_general(a, b, (((1,), (0,)), ((), ())), preferred_element_type=F32)


def dot_nt(a, b):
    return lax.dot_general(a, b, (((1,), (1,)), ((), ())), preferred_element_type=F32)


def lagrange(coord):
    values = []
    slopes = []
    for which in range(4):
        others = [NODE_POINTS[j] for j in range(4) if j != which]
        denom = 1.0
        for other in others:
            denom = denom * (NODE_POINTS[which] - other)
        first = coord - others[0]
        second = coord - others[1]
        third = coord - others[2]
        scale = 1.0 / denom
        values.append(first * second * third * scale)
        slopes.append((second * third + first * third + first * second) * scale)
    return values, slopes


def pick(rows, index):
    out = jnp.where(index == 0, rows[0], rows[1])
    return jnp.where(index < 2, out, jnp.where(index == 2, rows[2], rows[3]))


def deformed(strain, grad):
    form = [[strain[k * 3 + l] + (1.0 if k == l else 0.0) for l in range(3)] for k in range(3)]
    return [
        [
            form[k][l]
            + TIME_STEP * (grad[k * 3] * form[0][l] + grad[k * 3 + 1] * form[1][l] + grad[k * 3 + 2] * form[2][l])
            for l in range(3)
        ]
        for k in range(3)
    ]


def stiffness():
    row, col = iota((64, 64), 0), iota((64, 64), 1)
    total = jnp.where(row == col, 6.0, 0.0)
    for step in (16, 4, 1):
        place_row, place_col = (row // step) % 4, (col // step) % 4
        same = (row - place_row * step) == (col - place_col * step)
        near = jnp.abs(place_row - place_col) == 1
        total = total - jnp.where(same & near, 1.0, 0.0)
    return total


def left_operand(stack):
    high, low = split(stack)
    return jnp.concatenate([high, high, low], axis=1)


def constrain(field, left, config):
    high, low = split(field)
    product = dot(left, jnp.concatenate([high, low, high], axis=0))
    total = field
    for which in range(8):
        total = total + jnp.where(config == which, product[which * 64 : which * 64 + 64], 0.0)
    return total


def kernel(
    vel_hbm, visc_hbm, config_hbm, offsets_hbm, cells_hbm, coords_hbm, strain_hbm, motion_hbm,
    fluid, deform,
    vel, visc, config, offsets, cells, items,
    slot_device, field, halves, applied, onehot, shapes, nodal, results, turned, grads,
    packet, middle, arrived, reply, reply_middle, reply_arrived, reply_turned,
    edge, low_x, high_x, low_y, high_y, low_z, high_z,
    in_sem, own_sem, entered_x, entered_y, entered_s,
    send_a, recv_a, send_b, recv_b, send_c, recv_c, send_d, recv_d, send_h, recv_h,
):
    me_x, me_y, me_s = lax.axis_index("dx"), lax.axis_index("dy"), lax.axis_index("solid")

    loads = [
        pltpu.make_async_copy(source, target, in_sem.at[which])
        for which, (source, target) in enumerate(
            (
                (strain_hbm, items.at[0:72]),
                (motion_hbm, items.at[72:96]),
                (coords_hbm, items.at[96:120]),
                (cells_hbm, cells),
                (vel_hbm, vel),
                (offsets_hbm, offsets),
                (config_hbm, config),
                (visc_hbm, visc),
            )
        )
    ]
    for load in loads:
        load.start()

    def rank(place):
        return jnp.where(place < 4, place, 11 - place)

    def later_s(step):
        return rank(lax.rem(me_s + step, N_SOLID)) > rank(me_s)

    barrier = pltpu.get_barrier_semaphore()
    for step in range(1, N_DY):

        @pl.when(me_y + step < N_DY)
        def _():
            pl.semaphore_signal(barrier, inc=1, device_id={"dy": me_y + step}, device_id_type=MESH)

    for step in range(1, N_SOLID):

        @pl.when(later_s(step))
        def _():
            pl.semaphore_signal(barrier, inc=1, device_id={"solid": lax.rem(me_s + step, N_SOLID)}, device_id_type=MESH)

    up_x, down_x = lax.rem(me_x + 1, N_DX), lax.rem(me_x + N_DX - 1, N_DX)
    for peer in (up_x, down_x):

        @pl.when(peer > me_x)
        def _():
            pl.semaphore_signal(barrier, inc=1, device_id={"dx": peer}, device_id_type=MESH)

    def over_solid(source, target, send, recv, own):
        copies = [pltpu.make_async_copy(source.at[:, me_s], target.at[:, me_s], own)]
        for step in range(1, N_SOLID):
            peer = lax.rem(me_s + step, N_SOLID)
            copies.append(
                pltpu.make_async_remote_copy(
                    src_ref=source.at[:, peer],
                    dst_ref=target.at[:, me_s],
                    send_sem=send.at[step - 1],
                    recv_sem=recv.at[step - 1],
                    device_id={"solid": peer},
                    device_id_type=MESH,
                )
            )
        return copies

    def over_dy(source, target, send, recv, own):
        copies = [pltpu.make_async_copy(source.at[me_y], target.at[me_y], own)]
        for step in range(1, N_DY):
            peer = lax.rem(me_y + step, N_DY)
            copies.append(
                pltpu.make_async_remote_copy(
                    src_ref=source.at[peer],
                    dst_ref=target.at[me_y],
                    send_sem=send.at[step - 1],
                    recv_sem=recv.at[step - 1],
                    device_id={"dy": peer},
                    device_id_type=MESH,
                )
            )
        return copies

    def start(copies):
        for copy in copies:
            copy.start()

    def start_early(copies):
        copies[0].start()
        for step in range(1, N_DY):

            @pl.when(me_y + step >= N_DY)
            def _():
                copies[step].start()

    def start_late(groups):
        for step in range(1, N_DY):

            @pl.when(me_y + step < N_DY)
            def _():
                pl.semaphore_wait(entered_y.at[step - 1], 1)
                for copies in groups:
                    copies[step].start()

    def greet_x():
        for which, peer in enumerate((up_x, down_x)):

            @pl.when(peer > me_x)
            def _():
                pl.semaphore_wait(entered_x.at[which], 1)

    def greet_s():
        for step in range(1, N_SOLID):

            @pl.when(later_s(step))
            def _():
                pl.semaphore_wait(entered_s.at[step - 1], 1)

    def arrive(copies):
        copies[0].wait()
        for copy in copies[1:]:
            copy.wait_recv()

    slot_place = iota((1, 1024), 1) & 7
    slot_device[...] = jnp.where((iota((1024, 128), 0) >> 3) == iota((1024, 128), 1), 1.0, 0.0).astype(BF16)
    reply_turned[...] = jnp.zeros_like(reply_turned)
    for load in loads[:4]:
        load.wait()
    items[120:128, :] = cells[...].astype(F32)
    rows = jnp.concatenate([items[pl.ds(g, 16, stride=8), :] for g in range(8)], axis=1)
    spread = jnp.concatenate([jnp.where(slot_place == c, rows, 0.0) for c in range(8)], axis=0)
    spread_high, spread_low = split(spread)
    packed = dot(spread_high, slot_device[...]) + dot(spread_low, slot_device[...])
    packet[...] = packed.T.reshape(16, 8, 128)
    turned[...] = packed

    earlier_x = jnp.where(me_x > 0, 1, 0) + jnp.where(me_x == N_DX - 1, 1, 0)
    earlier = me_y + rank(me_s) + earlier_x

    @pl.when(earlier > 0)
    def _():
        pl.semaphore_wait(barrier, earlier)

    first = over_dy(packet, middle, send_a, recv_a, own_sem.at[0])
    start_early(first)
    for step in range(1, N_DY):

        @pl.when(me_y >= step)
        def _():
            pl.semaphore_signal(entered_y.at[step - 1], inc=1, device_id={"dy": me_y - step}, device_id_type=MESH)

    for step in range(1, N_SOLID):

        @pl.when(jnp.logical_not(later_s(step)))
        def _():
            pl.semaphore_signal(
                entered_s.at[N_SOLID - 1 - step],
                inc=1,
                device_id={"solid": lax.rem(me_s + step, N_SOLID)},
                device_id_type=MESH,
            )

    for which, peer in enumerate((down_x, up_x)):

        @pl.when(peer < me_x)
        def _():
            pl.semaphore_signal(entered_x.at[which], inc=1, device_id={"dx": peer}, device_id_type=MESH)


    for load in loads[4:]:
        load.wait()
    own_config = config[...]
    config_row = jnp.concatenate([own_config[y : y + 1] for y in range(4)], axis=1)
    left = left_operand(offsets[...].reshape(512, 64))
    for k in range(3):
        start_field = jnp.concatenate([vel[pl.ds(k * 256 + y, 64, stride=4), :] for y in range(4)], axis=1)
        own = constrain(start_field, left, config_row)
        field[k] = own.reshape(4, 16, 512)
        high, low = split(own)
        halves[k * 64 : k * 64 + 64] = high
        halves[192 + k * 64 : 192 + k * 64 + 64] = low

    points = [turned[pl.ds(12 + j, 8, stride=16), :] for j in range(3)]
    target = turned[pl.ds(15, 8, stride=16), :]
    polys = [lagrange(point) for point in points]
    cell_index = iota((512, 256), 0).astype(F32)
    node_row = iota((16, 256), 0)
    for pair in range(4):
        lanes = slice(pair * 256, pair * 256 + 256)

        def row(x):
            return jnp.concatenate([x[2 * pair : 2 * pair + 1], x[2 * pair + 1 : 2 * pair + 2]], axis=1)

        onehot[:, lanes] = jnp.where(cell_index == row(target), 1.0, 0.0).astype(BF16)
        value_x, slope_x = [[row(x) for x in part] for part in polys[0]]
        value_y, slope_y = [pick([row(x) for x in part], node_row >> 2) for part in polys[1]]
        value_z, slope_z = [pick([row(x) for x in part], node_row & 3) for part in polys[2]]
        plain, along_y, along_z = value_y * value_z, slope_y * value_z, value_y * slope_z
        for a in range(4):
            at = slice(a * 16, a * 16 + 16)
            shapes[0, at, lanes] = value_x[a] * plain
            shapes[1, at, lanes] = slope_x[a] * plain
            shapes[2, at, lanes] = value_x[a] * along_y
            shapes[3, at, lanes] = value_x[a] * along_z
        gathered = dot(halves[...], onehot[:, lanes])
        for k in range(3):
            nodes = gathered[k * 64 : k * 64 + 64] + gathered[192 + k * 64 : 192 + k * 64 + 64]
            for j in range(4):
                total = jnp.sum(nodes * shapes[j, :, lanes], axis=0, keepdims=True)
                line = (k * 4 + j) * 8 + 2 * pair
                results[line : line + 1, :] = total[:, :128]
                results[line + 1 : line + 2, :] = total[:, 128:]
    seen = [results[q * 8 : q * 8 + 8, :] for q in range(12)]
    for k in range(3):
        for j in range(3):
            reply_turned[pl.ds(k * 3 + j, 8, stride=16), :] = seen[k * 4 + 1 + j]
    reply[...] = reply_turned[...].T.reshape(16, 8, 128)
    second = over_dy(reply, reply_middle, send_c, recv_c, own_sem.at[2])
    start_early(second)

    def remote(source, target, which, where):
        return pltpu.make_async_remote_copy(
            src_ref=source, dst_ref=target, send_sem=send_h.at[which], recv_sem=recv_h.at[which],
            device_id=where, device_id_type=MESH,
        )

    up_y, down_y = lax.rem(me_y + 1, N_DY), lax.rem(me_y + N_DY - 1, N_DY)
    up_s, down_s = lax.rem(me_s + 1, N_SOLID), lax.rem(me_s + N_SOLID - 1, N_SOLID)
    halo = [
        remote(field.at[:, 3], low_x, 0, {"dx": up_x}),
        remote(field.at[:, 0], high_x, 1, {"dx": down_x}),
        remote(field.at[:, :, 8:16, 384:512], low_y, 2, {"dy": up_y}),
        remote(field.at[:, :, 0:8, 0:128], high_y, 3, {"dy": down_y}),
        remote(edge.at[0], low_z, 4, {"solid": up_s}),
        remote(edge.at[1], high_z, 5, {"solid": down_s}),
    ]
    edge_row, edge_col = iota((16, 512), 0), iota((16, 512), 1)
    lane_edge = jnp.where(edge_row < 8, 127, 0)
    edge_pick = jnp.where(
        (edge_col == (edge_row & 7) * 128 + lane_edge) & ((edge_row & 7) < 4), 1.0, 0.0
    ).astype(BF16)
    edges = dot_nt(edge_pick, halves[0:192]) + dot_nt(edge_pick, halves[192:384])
    edge[...] = edges.reshape(2, 8, 192)

    own_visc = visc[...]
    visc_row = jnp.concatenate([own_visc[y : y + 1] for y in range(4)], axis=1)
    stiff = stiffness().astype(BF16)
    stiff = jnp.concatenate([stiff, stiff], axis=1)
    node = iota((64, 512), 0)
    ends = jnp.zeros((64, 512), F32)
    for step in (16, 4, 1):
        place = (node // step) % 4
        ends = ends + jnp.where((place == 0) | (place == 3), PENALTY, 0.0)
    for k in range(3):
        both = jnp.concatenate([halves[k * 64 : k * 64 + 64], halves[192 + k * 64 : 192 + k * 64 + 64]], axis=0)
        own = field[k].reshape(64, 512)
        applied[k] = (own * (1.0 + ends) + visc_row * dot(stiff, both)).reshape(4, 16, 512)

    start_late([first, second])
    greet_x()
    greet_s()
    start(halo)
    arrive(first)
    third = over_solid(middle, arrived, send_b, recv_b, own_sem.at[1])
    start(third)
    arrive(second)
    fourth = over_solid(reply_middle, reply_arrived, send_d, recv_d, own_sem.at[3])
    start(fourth)

    for copy in halo:
        copy.wait_recv()
    flipped = left_operand(jnp.concatenate([offsets[w].T for w in range(8)], axis=0))
    edge_lane = iota((32, 512), 1)
    edge_line = iota((32, 512), 0)
    edge_place = jnp.where(
        (edge_lane == (edge_line & 7) * 128 + jnp.where((edge_line & 8) == 0, 0, 127)) & ((edge_line & 7) < 4), 1.0, 0.0
    ).astype(BF16)
    below = jnp.where(me_s > 0, low_z[...], 0.0)
    above = jnp.where(me_s < N_SOLID - 1, high_z[...], 0.0)
    edge_high, edge_low = split(jnp.concatenate([below, above], axis=0).T)
    beside = dot(jnp.concatenate([edge_high, edge_low], axis=1), edge_place)
    lane = iota((64, 512), 1) & 127
    place_z = iota((64, 512), 0) & 3
    half_row = iota((4, 8, 512), 1)
    for k in range(3):
        own = field[k]
        flat = own.reshape(64, 512)
        outer = beside[k * 64 : k * 64 + 64]
        previous = jnp.concatenate([pltpu.roll(flat[:, y * 128 : y * 128 + 128], 1, 1) for y in range(4)], axis=1)
        following = jnp.concatenate([pltpu.roll(flat[:, y * 128 : y * 128 + 128], 127, 1) for y in range(4)], axis=1)
        previous = jnp.where(lane == 0, outer, previous)
        following = jnp.where(lane == 127, outer, following)
        near = jnp.where(place_z == 0, pltpu.roll(previous, 61, 0), 0.0)
        near = near + jnp.where(place_z == 3, pltpu.roll(following, 3, 0), 0.0)
        near = near.reshape(4, 16, 512)
        lower = jnp.concatenate([jnp.where(me_y > 0, low_y[k], 0.0), own[:, 8:16, :384]], axis=2)
        upper = jnp.concatenate([own[:, 0:8, 128:], jnp.where(me_y < N_DY - 1, high_y[k], 0.0)], axis=2)
        lower = jnp.where(half_row < 4, pltpu.roll(lower, 4, 1), 0.0)
        upper = jnp.where(half_row >= 4, pltpu.roll(upper, 4, 1), 0.0)
        near = near + jnp.concatenate([lower, upper], axis=1)
        lower = jnp.where(me_x > 0, low_x[k], 0.0)[None]
        upper = jnp.where(me_x < N_DX - 1, high_x[k], 0.0)[None]
        near = near + jnp.concatenate([lower, jnp.zeros((2, 16, 512), F32), upper], axis=0)
        applied[k] = applied[k] - PENALTY * near
    device_slot = jnp.where((iota((256, 1024), 1) >> 3) == (iota((256, 1024), 0) & 127), 1.0, 0.0).astype(BF16)

    arrive(third)
    turned[...] = arrived[...].reshape(128, 128).T
    moved = deformed(
        [turned[pl.ds(r, 8, stride=16), :] for r in range(9)],
        [seen[k * 4 + 1 + j] for k in range(3) for j in range(3)],
    )
    motion = [turned[pl.ds(9 + r, 8, stride=16), :] for r in range(3)]
    stress = {}
    for k in range(3):
        for m in range(k, 3):
            value = moved[k][0] * moved[m][0] + moved[k][1] * moved[m][1] + moved[k][2] * moved[m][2]
            stress[k, m] = stress[m, k] = value - 1.0 if k == m else value
    drag = [SPRING_RATE * (motion[k] - seen[k * 4]) for k in range(3)]
    for pair in range(4):
        lanes = slice(pair * 256, pair * 256 + 256)

        def row(x):
            return jnp.concatenate([x[2 * pair : 2 * pair + 1], x[2 * pair + 1 : 2 * pair + 2]], axis=1)

        for k in range(3):
            node_force = row(drag[k]) * shapes[0, :, lanes]
            for j in range(3):
                node_force = node_force - row(stress[k, j]) * shapes[1 + j, :, lanes]
            high, low = split(node_force)
            nodal[k * 64 : k * 64 + 64, lanes] = high
            nodal[192 + k * 64 : 192 + k * 64 + 64, lanes] = low
    force = dot_nt(nodal[...], onehot[...])
    for k in range(3):
        total = applied[k].reshape(64, 512)
        total = total - force[k * 64 : k * 64 + 64] - force[192 + k * 64 : 192 + k * 64 + 64]
        result = constrain(total, flipped, config_row)
        for y in range(4):
            fluid[pl.ds(k * 256 + y, 64, stride=4), :] = result[:, y * 128 : y * 128 + 128]

    arrive(fourth)
    back_high, back_low = split(reply_arrived[...].reshape(128, 128).T)
    wide = dot(jnp.concatenate([back_high, back_low], axis=1), device_slot)
    slots = jnp.zeros((16, 1024), F32)
    for c in range(8):
        slots = slots + jnp.where(slot_place == c, wide[c * 16 : c * 16 + 16], 0.0)
    for g in range(8):
        grads[pl.ds(g, 16, stride=8), :] = slots[:, g * 128 : g * 128 + 128]
    moved = deformed(
        [items[r * 8 : r * 8 + 8, :] for r in range(9)],
        [grads[r * 8 : r * 8 + 8, :] for r in range(9)],
    )
    for k in range(3):
        for l in range(3):
            deform[(k * 3 + l) * 8 : (k * 3 + l) * 8 + 8, :] = moved[k][l]
    for copies in (first, second, third, fourth):
        for copy in copies[1:]:
            copy.wait_send()
    for copy in halo:
        copy.wait_send()


def place_kernel(fluid, deform, fluid_hbm, deform_hbm, sem):
    copies = [
        pltpu.make_async_copy(fluid, fluid_hbm, sem.at[0]),
        pltpu.make_async_copy(deform, deform_hbm, sem.at[1]),
    ]
    for copy in copies:
        copy.start()
    for copy in copies:
        copy.wait()


def shards(velocity, viscosity, cell_config, constraint_offsets, slot_cells, point_coords, strain_offsets, solid_velocity):
    anywhere = pl.BlockSpec(memory_space=pl.ANY)
    inside = pl.BlockSpec(memory_space=pltpu.VMEM)
    vmem = pltpu.VMEM
    dma = pltpu.SemaphoreType.DMA
    fluid, deform = pl.pallas_call(
        kernel,
        out_shape=(vmem((768, 128), F32), vmem((72, 128), F32)),
        in_specs=[anywhere] * 8,
        out_specs=(inside, inside),
        scratch_shapes=[
            vmem((768, 128), F32),
            vmem((4, 128), F32),
            vmem((4, 128), jnp.int32),
            vmem((8, 64, 64), F32),
            vmem((8, 128), jnp.int32),
            vmem((128, 128), F32),
            vmem((1024, 128), BF16),
            vmem((3, 4, 16, 512), F32),
            vmem((384, 512), BF16),
            vmem((3, 4, 16, 512), F32),
            vmem((512, 1024), BF16),
            vmem((4, 64, 1024), F32),
            vmem((384, 1024), BF16),
            vmem((96, 128), F32),
            vmem((128, 128), F32),
            vmem((128, 128), F32),
            vmem((16, 8, 128), F32),
            vmem((16, 8, 128), F32),
            vmem((16, 8, 128), F32),
            vmem((16, 8, 128), F32),
            vmem((16, 8, 128), F32),
            vmem((16, 8, 128), F32),
            vmem((128, 128), F32),
            vmem((2, 8, 192), F32),
            vmem((3, 16, 512), F32),
            vmem((3, 16, 512), F32),
            vmem((3, 4, 8, 128), F32),
            vmem((3, 4, 8, 128), F32),
            vmem((8, 192), F32),
            vmem((8, 192), F32),
            dma((8,)),
            dma((4,)),
            pltpu.SemaphoreType.REGULAR((2,)),
            pltpu.SemaphoreType.REGULAR((N_DY - 1,)),
            pltpu.SemaphoreType.REGULAR((N_SOLID - 1,)),
            dma((N_DY - 1,)),
            dma((N_DY - 1,)),
            dma((N_SOLID - 1,)),
            dma((N_SOLID - 1,)),
            dma((N_DY - 1,)),
            dma((N_DY - 1,)),
            dma((N_SOLID - 1,)),
            dma((N_SOLID - 1,)),
            dma((6,)),
            dma((6,)),
        ],
        compiler_params=pltpu.CompilerParams(collective_id=0, has_side_effects=True),
    )(
        velocity.reshape(768, 128),
        viscosity.reshape(4, 128),
        cell_config.reshape(4, 128),
        constraint_offsets,
        slot_cells.reshape(8, 128),
        point_coords.reshape(24, 128),
        strain_offsets.reshape(72, 128),
        solid_velocity.reshape(24, 128),
    )
    fluid, deform = pl.pallas_call(
        place_kernel,
        out_shape=(jax.ShapeDtypeStruct((768, 128), F32), jax.ShapeDtypeStruct((72, 128), F32)),
        in_specs=[inside, inside],
        out_specs=(anywhere, anywhere),
        scratch_shapes=[dma((2,))],
    )(pltpu.with_memory_space_constraint(fluid, pltpu.VMEM), pltpu.with_memory_space_constraint(deform, pltpu.VMEM))
    return fluid.reshape(velocity.shape), deform.reshape(strain_offsets.shape)


def solution(mesh):
    return jax.shard_map(
        shards,
        mesh=mesh,
        in_specs=(
            P(None, None, None, None, "dx", "dy", "solid"),
            P("dx", "dy", "solid"),
            P("dx", "dy", "solid"),
            P(),
            P("dx", ("dy", "solid"), None),
            P(None, "dx", ("dy", "solid"), None),
            P(None, None, "dx", ("dy", "solid"), None),
            P(None, "dx", ("dy", "solid"), None),
        ),
        out_specs=(
            P(None, None, None, None, "dx", "dy", "solid"),
            P(None, None, "dx", ("dy", "solid"), None),
        ),
        check_vma=False,
    )
```

```python
import jax
import jax.numpy as jnp
from jax import lax
from jax.experimental import pallas as pl
from jax.experimental.pallas import tpu as pltpu
from jax.sharding import PartitionSpec as P

F32 = jnp.float32
BF16 = jnp.bfloat16
TIME_STEP = 0.05
SPRING_RATE = 2.0
PENALTY = 4.0
NODE_POINTS = (0.0, 1.0 / 3.0, 2.0 / 3.0, 1.0)
N_DX, N_DY, N_SOLID = 4, 16, 8
MESH = pl.DeviceIdType.MESH


def iota(shape, dim):
    return lax.broadcasted_iota(jnp.int32, shape, dim)


def split(x):
    high = x.astype(BF16)
    return high, (x - high.astype(F32)).astype(BF16)


def dot(a, b):
    return lax.dot_general(a, b, (((1,), (0,)), ((), ())), preferred_element_type=F32)


def dot_nt(a, b):
    return lax.dot_general(a, b, (((1,), (1,)), ((), ())), preferred_element_type=F32)


def lagrange(coord):
    values = []
    slopes = []
    for which in range(4):
        others = [NODE_POINTS[j] for j in range(4) if j != which]
        denom = 1.0
        for other in others:
            denom = denom * (NODE_POINTS[which] - other)
        first = coord - others[0]
        second = coord - others[1]
        third = coord - others[2]
        scale = 1.0 / denom
        values.append(first * second * third * scale)
        slopes.append((second * third + first * third + first * second) * scale)
    return values, slopes


def pick(rows, index):
    out = jnp.where(index == 0, rows[0], rows[1])
    return jnp.where(index < 2, out, jnp.where(index == 2, rows[2], rows[3]))


def deformed(strain, grad):
    form = [[strain[k * 3 + l] + (1.0 if k == l else 0.0) for l in range(3)] for k in range(3)]
    return [
        [
            form[k][l]
            + TIME_STEP * (grad[k * 3] * form[0][l] + grad[k * 3 + 1] * form[1][l] + grad[k * 3 + 2] * form[2][l])
            for l in range(3)
        ]
        for k in range(3)
    ]


def stiffness():
    row, col = iota((64, 64), 0), iota((64, 64), 1)
    total = jnp.where(row == col, 6.0, 0.0)
    for step in (16, 4, 1):
        place_row, place_col = (row // step) % 4, (col // step) % 4
        same = (row - place_row * step) == (col - place_col * step)
        near = jnp.abs(place_row - place_col) == 1
        total = total - jnp.where(same & near, 1.0, 0.0)
    return total


def left_operand(stack):
    high, low = split(stack)
    return jnp.concatenate([high, high, low], axis=1)


def constrain(field, left, config):
    high, low = split(field)
    product = dot(left, jnp.concatenate([high, low, high], axis=0))
    total = field
    for which in range(8):
        total = total + jnp.where(config == which, product[which * 64 : which * 64 + 64], 0.0)
    return total


def kernel(
    vel_hbm, visc_hbm, config_hbm, offsets_hbm, cells_hbm, coords_hbm, strain_hbm, motion_hbm,
    fluid, deform,
    vel, visc, config, offsets, cells, items,
    slot_device, field, halves, applied, onehot, shapes, nodal, results, turned, grads,
    packet, middle, arrived, reply, reply_middle, reply_arrived, reply_turned,
    edge, sides_x, sides_y, sides_z,
    in_sem, entered_x, entered_y, entered_s, sends, recvs,
):
    me_x, me_y, me_s = lax.axis_index("dx"), lax.axis_index("dy"), lax.axis_index("solid")

    small_loads = [
        pltpu.make_async_copy(strain_hbm, items.at[0:72], in_sem.at[0]),
        pltpu.make_async_copy(motion_hbm, items.at[72:96], in_sem.at[0]),
        pltpu.make_async_copy(coords_hbm, items.at[96:120], in_sem.at[0]),
    ]
    loads = [
        pltpu.make_async_copy(cells_hbm, cells, in_sem.at[1]),
        pltpu.make_async_copy(vel_hbm, vel, in_sem.at[2]),
        pltpu.make_async_copy(offsets_hbm, offsets, in_sem.at[3]),
        pltpu.make_async_copy(config_hbm, config, in_sem.at[4]),
        pltpu.make_async_copy(visc_hbm, visc, in_sem.at[5]),
    ]
    for load in small_loads + loads:
        load.start()

    def rank(place):
        return jnp.where(place < 4, place, 11 - place)

    def later_s(step):
        return rank(lax.rem(me_s + step, N_SOLID)) > rank(me_s)

    barrier = pltpu.get_barrier_semaphore()
    for step in range(1, N_DY):

        @pl.when(me_y + step < N_DY)
        def _():
            pl.semaphore_signal(barrier, inc=1, device_id={"dy": me_y + step}, device_id_type=MESH)

    for step in range(1, N_SOLID):

        @pl.when(later_s(step))
        def _():
            pl.semaphore_signal(barrier, inc=1, device_id={"solid": lax.rem(me_s + step, N_SOLID)}, device_id_type=MESH)

    up_x, down_x = lax.rem(me_x + 1, N_DX), lax.rem(me_x + N_DX - 1, N_DX)
    for peer in (up_x, down_x):

        @pl.when(peer > me_x)
        def _():
            pl.semaphore_signal(barrier, inc=1, device_id={"dx": peer}, device_id_type=MESH)

    def over_solid(source, target, send, recv):
        copies = [pltpu.make_async_copy(source.at[:, me_s], target.at[:, me_s], recv)]
        for step in range(1, N_SOLID):
            peer = lax.rem(me_s + step, N_SOLID)
            copies.append(
                pltpu.make_async_remote_copy(
                    src_ref=source.at[:, peer],
                    dst_ref=target.at[:, me_s],
                    send_sem=send,
                    recv_sem=recv,
                    device_id={"solid": peer},
                    device_id_type=MESH,
                )
            )
        return copies

    def over_dy(source, target, send, recv):
        copies = [pltpu.make_async_copy(source.at[me_y], target.at[me_y], recv)]
        for step in range(1, N_DY):
            peer = lax.rem(me_y + step, N_DY)
            copies.append(
                pltpu.make_async_remote_copy(
                    src_ref=source.at[peer],
                    dst_ref=target.at[me_y],
                    send_sem=send,
                    recv_sem=recv,
                    device_id={"dy": peer},
                    device_id_type=MESH,
                )
            )
        return copies

    def start(copies):
        for copy in copies:
            copy.start()

    def start_early(copies):
        copies[0].start()
        for step in range(1, N_DY):

            @pl.when(me_y + step >= N_DY)
            def _():
                copies[step].start()

    def start_late(groups):
        for batch in range(5):
            later = jnp.clip(N_DY - 1 - me_y - 3 * batch, 0, 3)

            @pl.when(later > 0)
            def _():
                pl.semaphore_wait(entered_y.at[batch], later)

            for step in range(3 * batch + 1, 3 * batch + 4):

                @pl.when(me_y + step < N_DY)
                def _():
                    for copies in groups:
                        copies[step].start()

    def greet(entered, later):
        @pl.when(later > 0)
        def _():
            pl.semaphore_wait(entered, later)

    def arrive(source, target, recv):
        pltpu.make_async_copy(source, target, recv).wait()

    slot_place = iota((1, 1024), 1) & 7
    slot_device[...] = jnp.where((iota((1024, 128), 0) >> 3) == iota((1024, 128), 1), 1.0, 0.0).astype(BF16)
    reply_turned[...] = jnp.zeros_like(reply_turned)
    pltpu.make_async_copy(items.at[0:120], items.at[0:120], in_sem.at[0]).wait()
    loads[0].wait()
    items[120:128, :] = cells[...].astype(F32)
    rows = jnp.concatenate([items[pl.ds(g, 16, stride=8), :] for g in range(8)], axis=1)
    spread = jnp.concatenate([jnp.where(slot_place == c, rows, 0.0) for c in range(8)], axis=0)
    spread_high, spread_low = split(spread)
    packed = dot(spread_high, slot_device[...]) + dot(spread_low, slot_device[...])
    packet[...] = packed.T.reshape(16, 8, 128)
    turned[...] = packed

    earlier_x = jnp.where(me_x > 0, 1, 0) + jnp.where(me_x == N_DX - 1, 1, 0)
    earlier = me_y + rank(me_s) + earlier_x

    @pl.when(earlier > 0)
    def _():
        pl.semaphore_wait(barrier, earlier)

    first = over_dy(packet, middle, sends.at[0], recvs.at[0])
    start_early(first)
    for step in range(1, N_DY):

        @pl.when(me_y >= step)
        def _():
            pl.semaphore_signal(entered_y.at[(step - 1) // 3], inc=1, device_id={"dy": me_y - step}, device_id_type=MESH)

    for step in range(1, N_SOLID):

        @pl.when(jnp.logical_not(later_s(step)))
        def _():
            pl.semaphore_signal(
                entered_s,
                inc=1,
                device_id={"solid": lax.rem(me_s + step, N_SOLID)},
                device_id_type=MESH,
            )

    for peer in (down_x, up_x):

        @pl.when(peer < me_x)
        def _():
            pl.semaphore_signal(entered_x, inc=1, device_id={"dx": peer}, device_id_type=MESH)


    for load in loads[1:]:
        load.wait()
    own_config = config[...]
    config_row = jnp.concatenate([own_config[y : y + 1] for y in range(4)], axis=1)
    left = left_operand(offsets[...].reshape(512, 64))
    for k in range(3):
        start_field = jnp.concatenate([vel[pl.ds(k * 256 + y, 64, stride=4), :] for y in range(4)], axis=1)
        own = constrain(start_field, left, config_row)
        field[k] = own.reshape(4, 16, 512)
        high, low = split(own)
        halves[k * 64 : k * 64 + 64] = high
        halves[192 + k * 64 : 192 + k * 64 + 64] = low

    points = [turned[pl.ds(12 + j, 8, stride=16), :] for j in range(3)]
    target = turned[pl.ds(15, 8, stride=16), :]
    polys = [lagrange(point) for point in points]
    cell_index = iota((512, 256), 0).astype(F32)
    node_row = iota((16, 256), 0)
    for pair in range(4):
        lanes = slice(pair * 256, pair * 256 + 256)

        def row(x):
            return jnp.concatenate([x[2 * pair : 2 * pair + 1], x[2 * pair + 1 : 2 * pair + 2]], axis=1)

        onehot[:, lanes] = jnp.where(cell_index == row(target), 1.0, 0.0).astype(BF16)
        value_x, slope_x = [[row(x) for x in part] for part in polys[0]]
        value_y, slope_y = [pick([row(x) for x in part], node_row >> 2) for part in polys[1]]
        value_z, slope_z = [pick([row(x) for x in part], node_row & 3) for part in polys[2]]
        plain, along_y, along_z = value_y * value_z, slope_y * value_z, value_y * slope_z
        for a in range(4):
            at = slice(a * 16, a * 16 + 16)
            shapes[0, at, lanes] = value_x[a] * plain
            shapes[1, at, lanes] = slope_x[a] * plain
            shapes[2, at, lanes] = value_x[a] * along_y
            shapes[3, at, lanes] = value_x[a] * along_z
        gathered = dot(halves[...], onehot[:, lanes])
        for k in range(3):
            nodes = gathered[k * 64 : k * 64 + 64] + gathered[192 + k * 64 : 192 + k * 64 + 64]
            for j in range(4):
                total = jnp.sum(nodes * shapes[j, :, lanes], axis=0, keepdims=True)
                line = (k * 4 + j) * 8 + 2 * pair
                results[line : line + 1, :] = total[:, :128]
                results[line + 1 : line + 2, :] = total[:, 128:]
    seen = [results[q * 8 : q * 8 + 8, :] for q in range(12)]
    for k in range(3):
        for j in range(3):
            reply_turned[pl.ds(k * 3 + j, 8, stride=16), :] = seen[k * 4 + 1 + j]
    reply[...] = reply_turned[...].T.reshape(16, 8, 128)
    second = over_dy(reply, reply_middle, sends.at[1], recvs.at[1])
    start_early(second)

    def remote(source, target, which, where):
        return pltpu.make_async_remote_copy(
            src_ref=source, dst_ref=target, send_sem=sends.at[which], recv_sem=recvs.at[which],
            device_id=where, device_id_type=MESH,
        )

    up_y, down_y = lax.rem(me_y + 1, N_DY), lax.rem(me_y + N_DY - 1, N_DY)
    up_s, down_s = lax.rem(me_s + 1, N_SOLID), lax.rem(me_s + N_SOLID - 1, N_SOLID)
    halo = [
        remote(field.at[:, 3], sides_x.at[0], 4, {"dx": up_x}),
        remote(field.at[:, 0], sides_x.at[1], 4, {"dx": down_x}),
        remote(field.at[:, :, 8:16, 384:512], sides_y.at[0], 5, {"dy": up_y}),
        remote(field.at[:, :, 0:8, 0:128], sides_y.at[1], 5, {"dy": down_y}),
        remote(edge.at[0], sides_z.at[0], 6, {"solid": up_s}),
        remote(edge.at[1], sides_z.at[1], 6, {"solid": down_s}),
    ]
    edge_row, edge_col = iota((16, 512), 0), iota((16, 512), 1)
    lane_edge = jnp.where(edge_row < 8, 127, 0)
    edge_pick = jnp.where(
        (edge_col == (edge_row & 7) * 128 + lane_edge) & ((edge_row & 7) < 4), 1.0, 0.0
    ).astype(BF16)
    edges = dot_nt(edge_pick, halves[0:192]) + dot_nt(edge_pick, halves[192:384])
    edge[...] = edges.reshape(2, 8, 192)

    own_visc = visc[...]
    visc_row = jnp.concatenate([own_visc[y : y + 1] for y in range(4)], axis=1)
    stiff = stiffness().astype(BF16)
    stiff = jnp.concatenate([stiff, stiff], axis=1)
    node = iota((64, 512), 0)
    ends = jnp.zeros((64, 512), F32)
    for step in (16, 4, 1):
        place = (node // step) % 4
        ends = ends + jnp.where((place == 0) | (place == 3), PENALTY, 0.0)
    for k in range(3):
        both = jnp.concatenate([halves[k * 64 : k * 64 + 64], halves[192 + k * 64 : 192 + k * 64 + 64]], axis=0)
        own = field[k].reshape(64, 512)
        applied[k] = (own * (1.0 + ends) + visc_row * dot(stiff, both)).reshape(4, 16, 512)

    start_late([first, second])
    greet(entered_x, 2 - earlier_x)
    greet(entered_s, N_SOLID - 1 - rank(me_s))
    start(halo)
    arrive(packet, middle, recvs.at[0])
    third = over_solid(middle, arrived, sends.at[2], recvs.at[2])
    start(third)
    arrive(reply, reply_middle, recvs.at[1])
    fourth = over_solid(reply_middle, reply_arrived, sends.at[3], recvs.at[3])
    start(fourth)

    arrive(sides_x, sides_x, recvs.at[4])
    arrive(sides_y, sides_y, recvs.at[5])
    arrive(sides_z, sides_z, recvs.at[6])
    flipped = left_operand(jnp.concatenate([offsets[w].T for w in range(8)], axis=0))
    edge_lane = iota((32, 512), 1)
    edge_line = iota((32, 512), 0)
    edge_place = jnp.where(
        (edge_lane == (edge_line & 7) * 128 + jnp.where((edge_line & 8) == 0, 0, 127)) & ((edge_line & 7) < 4), 1.0, 0.0
    ).astype(BF16)
    below = jnp.where(me_s > 0, sides_z[0], 0.0)
    above = jnp.where(me_s < N_SOLID - 1, sides_z[1], 0.0)
    edge_high, edge_low = split(jnp.concatenate([below, above], axis=0).T)
    beside = dot(jnp.concatenate([edge_high, edge_low], axis=1), edge_place)
    lane = iota((64, 512), 1) & 127
    place_z = iota((64, 512), 0) & 3
    half_row = iota((4, 8, 512), 1)
    for k in range(3):
        own = field[k]
        flat = own.reshape(64, 512)
        outer = beside[k * 64 : k * 64 + 64]
        previous = jnp.concatenate([pltpu.roll(flat[:, y * 128 : y * 128 + 128], 1, 1) for y in range(4)], axis=1)
        following = jnp.concatenate([pltpu.roll(flat[:, y * 128 : y * 128 + 128], 127, 1) for y in range(4)], axis=1)
        previous = jnp.where(lane == 0, outer, previous)
        following = jnp.where(lane == 127, outer, following)
        near = jnp.where(place_z == 0, pltpu.roll(previous, 61, 0), 0.0)
        near = near + jnp.where(place_z == 3, pltpu.roll(following, 3, 0), 0.0)
        near = near.reshape(4, 16, 512)
        lower = jnp.concatenate([jnp.where(me_y > 0, sides_y[0, k], 0.0), own[:, 8:16, :384]], axis=2)
        upper = jnp.concatenate([own[:, 0:8, 128:], jnp.where(me_y < N_DY - 1, sides_y[1, k], 0.0)], axis=2)
        lower = jnp.where(half_row < 4, pltpu.roll(lower, 4, 1), 0.0)
        upper = jnp.where(half_row >= 4, pltpu.roll(upper, 4, 1), 0.0)
        near = near + jnp.concatenate([lower, upper], axis=1)
        lower = jnp.where(me_x > 0, sides_x[0, k], 0.0)[None]
        upper = jnp.where(me_x < N_DX - 1, sides_x[1, k], 0.0)[None]
        near = near + jnp.concatenate([lower, jnp.zeros((2, 16, 512), F32), upper], axis=0)
        applied[k] = applied[k] - PENALTY * near
    device_slot = jnp.where((iota((256, 1024), 1) >> 3) == (iota((256, 1024), 0) & 127), 1.0, 0.0).astype(BF16)

    arrive(middle, arrived, recvs.at[2])
    turned[...] = arrived[...].reshape(128, 128).T
    moved = deformed(
        [turned[pl.ds(r, 8, stride=16), :] for r in range(9)],
        [seen[k * 4 + 1 + j] for k in range(3) for j in range(3)],
    )
    motion = [turned[pl.ds(9 + r, 8, stride=16), :] for r in range(3)]
    stress = {}
    for k in range(3):
        for m in range(k, 3):
            value = moved[k][0] * moved[m][0] + moved[k][1] * moved[m][1] + moved[k][2] * moved[m][2]
            stress[k, m] = stress[m, k] = value - 1.0 if k == m else value
    drag = [SPRING_RATE * (motion[k] - seen[k * 4]) for k in range(3)]
    for pair in range(4):
        lanes = slice(pair * 256, pair * 256 + 256)

        def row(x):
            return jnp.concatenate([x[2 * pair : 2 * pair + 1], x[2 * pair + 1 : 2 * pair + 2]], axis=1)

        for k in range(3):
            node_force = row(drag[k]) * shapes[0, :, lanes]
            for j in range(3):
                node_force = node_force - row(stress[k, j]) * shapes[1 + j, :, lanes]
            high, low = split(node_force)
            nodal[k * 64 : k * 64 + 64, lanes] = high
            nodal[192 + k * 64 : 192 + k * 64 + 64, lanes] = low
    force = dot_nt(nodal[...], onehot[...])
    for k in range(3):
        total = applied[k].reshape(64, 512)
        total = total - force[k * 64 : k * 64 + 64] - force[192 + k * 64 : 192 + k * 64 + 64]
        result = constrain(total, flipped, config_row)
        for y in range(4):
            fluid[pl.ds(k * 256 + y, 64, stride=4), :] = result[:, y * 128 : y * 128 + 128]

    arrive(reply_middle, reply_arrived, recvs.at[3])
    back_high, back_low = split(reply_arrived[...].reshape(128, 128).T)
    wide = dot(jnp.concatenate([back_high, back_low], axis=1), device_slot)
    slots = jnp.zeros((16, 1024), F32)
    for c in range(8):
        slots = slots + jnp.where(slot_place == c, wide[c * 16 : c * 16 + 16], 0.0)
    for g in range(8):
        grads[pl.ds(g, 16, stride=8), :] = slots[:, g * 128 : g * 128 + 128]
    moved = deformed(
        [items[r * 8 : r * 8 + 8, :] for r in range(9)],
        [grads[r * 8 : r * 8 + 8, :] for r in range(9)],
    )
    for k in range(3):
        for l in range(3):
            deform[(k * 3 + l) * 8 : (k * 3 + l) * 8 + 8, :] = moved[k][l]
    arrive(packet.at[0:15], middle.at[0:15], sends.at[0])
    arrive(reply.at[0:15], reply_middle.at[0:15], sends.at[1])
    arrive(middle.at[0:14], arrived.at[0:14], sends.at[2])
    arrive(reply_middle.at[0:14], reply_arrived.at[0:14], sends.at[3])
    arrive(sides_x, sides_x, sends.at[4])
    arrive(sides_y, sides_y, sends.at[5])
    arrive(sides_z, sides_z, sends.at[6])


def place_kernel(fluid, deform, fluid_hbm, deform_hbm, sem):
    copies = [
        pltpu.make_async_copy(fluid, fluid_hbm, sem.at[0]),
        pltpu.make_async_copy(deform, deform_hbm, sem.at[1]),
    ]
    for copy in copies:
        copy.start()
    for copy in copies:
        copy.wait()


def shards(velocity, viscosity, cell_config, constraint_offsets, slot_cells, point_coords, strain_offsets, solid_velocity):
    anywhere = pl.BlockSpec(memory_space=pl.ANY)
    inside = pl.BlockSpec(memory_space=pltpu.VMEM)
    vmem = pltpu.VMEM
    dma = pltpu.SemaphoreType.DMA
    fluid, deform = pl.pallas_call(
        kernel,
        out_shape=(vmem((768, 128), F32), vmem((72, 128), F32)),
        in_specs=[anywhere] * 8,
        out_specs=(inside, inside),
        scratch_shapes=[
            vmem((768, 128), F32),
            vmem((4, 128), F32),
            vmem((4, 128), jnp.int32),
            vmem((8, 64, 64), F32),
            vmem((8, 128), jnp.int32),
            vmem((128, 128), F32),
            vmem((1024, 128), BF16),
            vmem((3, 4, 16, 512), F32),
            vmem((384, 512), BF16),
            vmem((3, 4, 16, 512), F32),
            vmem((512, 1024), BF16),
            vmem((4, 64, 1024), F32),
            vmem((384, 1024), BF16),
            vmem((96, 128), F32),
            vmem((128, 128), F32),
            vmem((128, 128), F32),
            vmem((16, 8, 128), F32),
            vmem((16, 8, 128), F32),
            vmem((16, 8, 128), F32),
            vmem((16, 8, 128), F32),
            vmem((16, 8, 128), F32),
            vmem((16, 8, 128), F32),
            vmem((128, 128), F32),
            vmem((2, 8, 192), F32),
            vmem((2, 3, 16, 512), F32),
            vmem((2, 3, 4, 8, 128), F32),
            vmem((2, 8, 192), F32),
            dma((6,)),
            pltpu.SemaphoreType.REGULAR,
            pltpu.SemaphoreType.REGULAR((5,)),
            pltpu.SemaphoreType.REGULAR,
            dma((7,)),
            dma((7,)),
        ],
        compiler_params=pltpu.CompilerParams(collective_id=0, has_side_effects=True),
    )(
        velocity.reshape(768, 128),
        viscosity.reshape(4, 128),
        cell_config.reshape(4, 128),
        constraint_offsets,
        slot_cells.reshape(8, 128),
        point_coords.reshape(24, 128),
        strain_offsets.reshape(72, 128),
        solid_velocity.reshape(24, 128),
    )
    fluid, deform = pl.pallas_call(
        place_kernel,
        out_shape=(jax.ShapeDtypeStruct((768, 128), F32), jax.ShapeDtypeStruct((72, 128), F32)),
        in_specs=[inside, inside],
        out_specs=(anywhere, anywhere),
        scratch_shapes=[dma((2,))],
    )(pltpu.with_memory_space_constraint(fluid, pltpu.VMEM), pltpu.with_memory_space_constraint(deform, pltpu.VMEM))
    return fluid.reshape(velocity.shape), deform.reshape(strain_offsets.shape)


def solution(mesh):
    return jax.shard_map(
        shards,
        mesh=mesh,
        in_specs=(
            P(None, None, None, None, "dx", "dy", "solid"),
            P("dx", "dy", "solid"),
            P("dx", "dy", "solid"),
            P(),
            P("dx", ("dy", "solid"), None),
            P(None, "dx", ("dy", "solid"), None),
            P(None, None, "dx", ("dy", "solid"), None),
            P(None, "dx", ("dy", "solid"), None),
        ),
        out_specs=(
            P(None, None, None, None, "dx", "dy", "solid"),
            P(None, None, "dx", ("dy", "solid"), None),
        ),
        check_vma=False,
    )
```

```python
import jax
import jax.numpy as jnp
from jax import lax
from jax.experimental import pallas as pl
from jax.experimental.pallas import tpu as pltpu
from jax.sharding import PartitionSpec as P

F32 = jnp.float32
BF16 = jnp.bfloat16
TIME_STEP = 0.05
SPRING_RATE = 2.0
PENALTY = 4.0
NODE_POINTS = (0.0, 1.0 / 3.0, 2.0 / 3.0, 1.0)
N_DX, N_DY, N_SOLID = 4, 16, 8
MESH = pl.DeviceIdType.MESH


def iota(shape, dim):
    return lax.broadcasted_iota(jnp.int32, shape, dim)


def split(x):
    high = x.astype(BF16)
    return high, (x - high.astype(F32)).astype(BF16)


def dot(a, b):
    return lax.dot_general(a, b, (((1,), (0,)), ((), ())), preferred_element_type=F32)


def dot_nt(a, b):
    return lax.dot_general(a, b, (((1,), (1,)), ((), ())), preferred_element_type=F32)


def lagrange(coord):
    values = []
    slopes = []
    for which in range(4):
        others = [NODE_POINTS[j] for j in range(4) if j != which]
        denom = 1.0
        for other in others:
            denom = denom * (NODE_POINTS[which] - other)
        first = coord - others[0]
        second = coord - others[1]
        third = coord - others[2]
        scale = 1.0 / denom
        values.append(first * second * third * scale)
        slopes.append((second * third + first * third + first * second) * scale)
    return values, slopes


def pick(rows, index):
    out = jnp.where(index == 0, rows[0], rows[1])
    return jnp.where(index < 2, out, jnp.where(index == 2, rows[2], rows[3]))


def deformed(strain, grad):
    form = [[strain[k * 3 + l] + (1.0 if k == l else 0.0) for l in range(3)] for k in range(3)]
    return [
        [
            form[k][l]
            + TIME_STEP * (grad[k * 3] * form[0][l] + grad[k * 3 + 1] * form[1][l] + grad[k * 3 + 2] * form[2][l])
            for l in range(3)
        ]
        for k in range(3)
    ]


def stiffness():
    row, col = iota((64, 64), 0), iota((64, 64), 1)
    total = jnp.where(row == col, 6.0, 0.0)
    for step in (16, 4, 1):
        place_row, place_col = (row // step) % 4, (col // step) % 4
        same = (row - place_row * step) == (col - place_col * step)
        near = jnp.abs(place_row - place_col) == 1
        total = total - jnp.where(same & near, 1.0, 0.0)
    return total


def left_operand(stack):
    high, low = split(stack)
    return jnp.concatenate([high, high, low], axis=1)


def constrain(field, left, config):
    high, low = split(field)
    product = dot(left, jnp.concatenate([high, low, high], axis=0))
    total = field
    for which in range(8):
        total = total + jnp.where(config == which, product[which * 64 : which * 64 + 64], 0.0)
    return total


def kernel(
    vel_hbm, visc_hbm, config_hbm, offsets_hbm, cells_hbm, coords_hbm, strain_hbm, motion_hbm,
    fluid, deform,
    vel, visc, config, offsets, cells, items,
    slot_device, field, halves, applied, onehot, shapes, nodal, results, turned, grads,
    packet, middle, arrived, reply, reply_middle, reply_arrived, reply_turned,
    edge, sides_x, sides_y, sides_z,
    in_sem, entered_x, entered_y, entered_s, sends, recvs,
):
    me_x, me_y, me_s = lax.axis_index("dx"), lax.axis_index("dy"), lax.axis_index("solid")

    small_loads = [
        pltpu.make_async_copy(strain_hbm, items.at[0:72], in_sem.at[0]),
        pltpu.make_async_copy(motion_hbm, items.at[72:96], in_sem.at[0]),
        pltpu.make_async_copy(coords_hbm, items.at[96:120], in_sem.at[0]),
    ]
    loads = [
        pltpu.make_async_copy(cells_hbm, cells, in_sem.at[1]),
        pltpu.make_async_copy(vel_hbm, vel, in_sem.at[2]),
        pltpu.make_async_copy(offsets_hbm, offsets, in_sem.at[3]),
        pltpu.make_async_copy(config_hbm, config, in_sem.at[4]),
        pltpu.make_async_copy(visc_hbm, visc, in_sem.at[5]),
    ]
    for load in small_loads + loads:
        load.start()

    def rank(place):
        return jnp.where(place < 4, place, 11 - place)

    def later_s(step):
        return rank(lax.rem(me_s + step, N_SOLID)) > rank(me_s)

    barrier = pltpu.get_barrier_semaphore()
    for step in range(1, N_DY):

        @pl.when(me_y + step < N_DY)
        def _():
            pl.semaphore_signal(barrier, inc=1, device_id={"dy": me_y + step}, device_id_type=MESH)

    for step in range(1, N_SOLID):

        @pl.when(later_s(step))
        def _():
            pl.semaphore_signal(barrier, inc=1, device_id={"solid": lax.rem(me_s + step, N_SOLID)}, device_id_type=MESH)

    up_x, down_x = lax.rem(me_x + 1, N_DX), lax.rem(me_x + N_DX - 1, N_DX)
    for peer in (up_x, down_x):

        @pl.when(peer > me_x)
        def _():
            pl.semaphore_signal(barrier, inc=1, device_id={"dx": peer}, device_id_type=MESH)

    def over_solid(source, target, send, recv):
        copies = [pltpu.make_async_copy(source.at[:, me_s], target.at[:, me_s], recv)]
        for step in range(1, N_SOLID):
            peer = lax.rem(me_s + step, N_SOLID)
            copies.append(
                pltpu.make_async_remote_copy(
                    src_ref=source.at[:, peer],
                    dst_ref=target.at[:, me_s],
                    send_sem=send,
                    recv_sem=recv,
                    device_id={"solid": peer},
                    device_id_type=MESH,
                )
            )
        return copies

    def over_dy(source, target, send, recv):
        copies = [pltpu.make_async_copy(source.at[me_y], target.at[me_y], recv)]
        for step in range(1, N_DY):
            peer = lax.rem(me_y + step, N_DY)
            copies.append(
                pltpu.make_async_remote_copy(
                    src_ref=source.at[peer],
                    dst_ref=target.at[me_y],
                    send_sem=send,
                    recv_sem=recv,
                    device_id={"dy": peer},
                    device_id_type=MESH,
                )
            )
        return copies

    def start(copies):
        for copy in copies:
            copy.start()

    def start_early(copies):
        copies[0].start()
        for step in range(1, N_DY):

            @pl.when(me_y + step >= N_DY)
            def _():
                copies[step].start()

    def start_late(groups):
        for batch in range(5):
            later = jnp.clip(N_DY - 1 - me_y - 3 * batch, 0, 3)

            @pl.when(later > 0)
            def _():
                pl.semaphore_wait(entered_y.at[batch], later)

            for step in range(3 * batch + 1, 3 * batch + 4):

                @pl.when(me_y + step < N_DY)
                def _():
                    for copies in groups:
                        copies[step].start()

    def greet(entered, later):
        @pl.when(later > 0)
        def _():
            pl.semaphore_wait(entered, later)

    def arrive(source, target, recv):
        pltpu.make_async_copy(source, target, recv).wait()

    slot_place = iota((1, 1024), 1) & 7
    slot_device[...] = jnp.where((iota((1024, 128), 0) >> 3) == iota((1024, 128), 1), 1.0, 0.0).astype(BF16)
    reply_turned[...] = jnp.zeros_like(reply_turned)
    pltpu.make_async_copy(items.at[0:120], items.at[0:120], in_sem.at[0]).wait()
    loads[0].wait()
    items[120:128, :] = cells[...].astype(F32)
    rows = jnp.concatenate([items[pl.ds(g, 16, stride=8), :] for g in range(8)], axis=1)
    spread = jnp.concatenate([jnp.where(slot_place == c, rows, 0.0) for c in range(8)], axis=0)
    spread_high, spread_low = split(spread)
    packed = dot(spread_high, slot_device[...]) + dot(spread_low, slot_device[...])
    packet[...] = packed.T.reshape(16, 8, 128)
    turned[...] = packed

    earlier_x = jnp.where(me_x > 0, 1, 0) + jnp.where(me_x == N_DX - 1, 1, 0)
    earlier = me_y + rank(me_s) + earlier_x

    @pl.when(earlier > 0)
    def _():
        pl.semaphore_wait(barrier, earlier)

    first = over_dy(packet, middle, sends.at[0], recvs.at[0])
    start_early(first)
    for step in range(1, N_DY):

        @pl.when(me_y >= step)
        def _():
            pl.semaphore_signal(entered_y.at[(step - 1) // 3], inc=1, device_id={"dy": me_y - step}, device_id_type=MESH)

    for load in loads[1:]:
        load.wait()
    own_config = config[...]
    config_row = jnp.concatenate([own_config[y : y + 1] for y in range(4)], axis=1)
    left = left_operand(offsets[...].reshape(512, 64))
    points = [turned[pl.ds(12 + j, 8, stride=16), :] for j in range(3)]
    target = turned[pl.ds(15, 8, stride=16), :]
    polys = [lagrange(point) for point in points]
    cell_index = iota((512, 256), 0).astype(F32)
    node_row = iota((16, 256), 0)

    def tables(pair):
        lanes = slice(pair * 256, pair * 256 + 256)

        def row(x):
            return jnp.concatenate([x[2 * pair : 2 * pair + 1], x[2 * pair + 1 : 2 * pair + 2]], axis=1)

        onehot[:, lanes] = jnp.where(cell_index == row(target), 1.0, 0.0).astype(BF16)
        value_x, slope_x = [[row(x) for x in part] for part in polys[0]]
        value_y, slope_y = [pick([row(x) for x in part], node_row >> 2) for part in polys[1]]
        value_z, slope_z = [pick([row(x) for x in part], node_row & 3) for part in polys[2]]
        plain, along_y, along_z = value_y * value_z, slope_y * value_z, value_y * slope_z
        for a in range(4):
            at = slice(a * 16, a * 16 + 16)
            shapes[0, at, lanes] = value_x[a] * plain
            shapes[1, at, lanes] = slope_x[a] * plain
            shapes[2, at, lanes] = value_x[a] * along_y
            shapes[3, at, lanes] = value_x[a] * along_z

    for k in range(3):
        start_field = jnp.concatenate([vel[pl.ds(k * 256 + y, 64, stride=4), :] for y in range(4)], axis=1)
        own = constrain(start_field, left, config_row)
        field[k] = own.reshape(4, 16, 512)
        high, low = split(own)
        halves[k * 64 : k * 64 + 64] = high
        halves[192 + k * 64 : 192 + k * 64 + 64] = low
    for pair in range(4):
        tables(pair)
        lanes = slice(pair * 256, pair * 256 + 256)
        gathered = dot(halves[...], onehot[:, lanes])
        for k in range(3):
            nodes = gathered[k * 64 : k * 64 + 64] + gathered[192 + k * 64 : 192 + k * 64 + 64]
            for j in range(4):
                total = jnp.sum(nodes * shapes[j, :, lanes], axis=0, keepdims=True)
                line = (k * 4 + j) * 8 + 2 * pair
                results[line : line + 1, :] = total[:, :128]
                results[line + 1 : line + 2, :] = total[:, 128:]
    seen = [results[q * 8 : q * 8 + 8, :] for q in range(12)]
    for k in range(3):
        for j in range(3):
            reply_turned[pl.ds(k * 3 + j, 8, stride=16), :] = seen[k * 4 + 1 + j]
    reply[...] = reply_turned[...].T.reshape(16, 8, 128)
    second = over_dy(reply, reply_middle, sends.at[1], recvs.at[1])
    start_early(second)
    for step in range(1, N_SOLID):

        @pl.when(jnp.logical_not(later_s(step)))
        def _():
            pl.semaphore_signal(
                entered_s,
                inc=1,
                device_id={"solid": lax.rem(me_s + step, N_SOLID)},
                device_id_type=MESH,
            )

    for peer in (down_x, up_x):

        @pl.when(peer < me_x)
        def _():
            pl.semaphore_signal(entered_x, inc=1, device_id={"dx": peer}, device_id_type=MESH)


    def remote(source, target, which, where):
        return pltpu.make_async_remote_copy(
            src_ref=source, dst_ref=target, send_sem=sends.at[which], recv_sem=recvs.at[which],
            device_id=where, device_id_type=MESH,
        )

    up_y, down_y = lax.rem(me_y + 1, N_DY), lax.rem(me_y + N_DY - 1, N_DY)
    up_s, down_s = lax.rem(me_s + 1, N_SOLID), lax.rem(me_s + N_SOLID - 1, N_SOLID)
    halo = [
        remote(field.at[:, 3], sides_x.at[0], 4, {"dx": up_x}),
        remote(field.at[:, 0], sides_x.at[1], 4, {"dx": down_x}),
        remote(field.at[:, :, 8:16, 384:512], sides_y.at[0], 5, {"dy": up_y}),
        remote(field.at[:, :, 0:8, 0:128], sides_y.at[1], 5, {"dy": down_y}),
        remote(edge.at[0], sides_z.at[0], 6, {"solid": up_s}),
        remote(edge.at[1], sides_z.at[1], 6, {"solid": down_s}),
    ]
    edge_row, edge_col = iota((16, 512), 0), iota((16, 512), 1)
    lane_edge = jnp.where(edge_row < 8, 127, 0)
    edge_pick = jnp.where(
        (edge_col == (edge_row & 7) * 128 + lane_edge) & ((edge_row & 7) < 4), 1.0, 0.0
    ).astype(BF16)
    edges = dot_nt(edge_pick, halves[0:192]) + dot_nt(edge_pick, halves[192:384])
    edge[...] = edges.reshape(2, 8, 192)

    own_visc = visc[...]
    visc_row = jnp.concatenate([own_visc[y : y + 1] for y in range(4)], axis=1)
    stiff = stiffness().astype(BF16)
    stiff = jnp.concatenate([stiff, stiff], axis=1)
    node = iota((64, 512), 0)
    ends = jnp.zeros((64, 512), F32)
    for step in (16, 4, 1):
        place = (node // step) % 4
        ends = ends + jnp.where((place == 0) | (place == 3), PENALTY, 0.0)
    for k in range(3):
        both = jnp.concatenate([halves[k * 64 : k * 64 + 64], halves[192 + k * 64 : 192 + k * 64 + 64]], axis=0)
        own = field[k].reshape(64, 512)
        applied[k] = (own * (1.0 + ends) + visc_row * dot(stiff, both)).reshape(4, 16, 512)

    start_late([first, second])
    greet(entered_x, 2 - earlier_x)
    greet(entered_s, N_SOLID - 1 - rank(me_s))
    start(halo)
    arrive(packet, middle, recvs.at[0])
    third = over_solid(middle, arrived, sends.at[2], recvs.at[2])
    start(third)
    arrive(reply, reply_middle, recvs.at[1])
    fourth = over_solid(reply_middle, reply_arrived, sends.at[3], recvs.at[3])
    start(fourth)

    arrive(sides_x, sides_x, recvs.at[4])
    arrive(sides_y, sides_y, recvs.at[5])
    arrive(sides_z, sides_z, recvs.at[6])
    flipped = left_operand(jnp.concatenate([offsets[w].T for w in range(8)], axis=0))
    edge_lane = iota((32, 512), 1)
    edge_line = iota((32, 512), 0)
    edge_place = jnp.where(
        (edge_lane == (edge_line & 7) * 128 + jnp.where((edge_line & 8) == 0, 0, 127)) & ((edge_line & 7) < 4), 1.0, 0.0
    ).astype(BF16)
    below = jnp.where(me_s > 0, sides_z[0], 0.0)
    above = jnp.where(me_s < N_SOLID - 1, sides_z[1], 0.0)
    edge_high, edge_low = split(jnp.concatenate([below, above], axis=0).T)
    beside = dot(jnp.concatenate([edge_high, edge_low], axis=1), edge_place)
    lane = iota((64, 512), 1) & 127
    place_z = iota((64, 512), 0) & 3
    half_row = iota((4, 8, 512), 1)
    for k in range(3):
        own = field[k]
        flat = own.reshape(64, 512)
        outer = beside[k * 64 : k * 64 + 64]
        previous = jnp.concatenate([pltpu.roll(flat[:, y * 128 : y * 128 + 128], 1, 1) for y in range(4)], axis=1)
        following = jnp.concatenate([pltpu.roll(flat[:, y * 128 : y * 128 + 128], 127, 1) for y in range(4)], axis=1)
        previous = jnp.where(lane == 0, outer, previous)
        following = jnp.where(lane == 127, outer, following)
        near = jnp.where(place_z == 0, pltpu.roll(previous, 61, 0), 0.0)
        near = near + jnp.where(place_z == 3, pltpu.roll(following, 3, 0), 0.0)
        near = near.reshape(4, 16, 512)
        lower = jnp.concatenate([jnp.where(me_y > 0, sides_y[0, k], 0.0), own[:, 8:16, :384]], axis=2)
        upper = jnp.concatenate([own[:, 0:8, 128:], jnp.where(me_y < N_DY - 1, sides_y[1, k], 0.0)], axis=2)
        lower = jnp.where(half_row < 4, pltpu.roll(lower, 4, 1), 0.0)
        upper = jnp.where(half_row >= 4, pltpu.roll(upper, 4, 1), 0.0)
        near = near + jnp.concatenate([lower, upper], axis=1)
        lower = jnp.where(me_x > 0, sides_x[0, k], 0.0)[None]
        upper = jnp.where(me_x < N_DX - 1, sides_x[1, k], 0.0)[None]
        near = near + jnp.concatenate([lower, jnp.zeros((2, 16, 512), F32), upper], axis=0)
        applied[k] = applied[k] - PENALTY * near
    device_slot = jnp.where((iota((256, 1024), 1) >> 3) == (iota((256, 1024), 0) & 127), 1.0, 0.0).astype(BF16)

    arrive(middle, arrived, recvs.at[2])
    turned[...] = arrived[...].reshape(128, 128).T
    moved = deformed(
        [turned[pl.ds(r, 8, stride=16), :] for r in range(9)],
        [seen[k * 4 + 1 + j] for k in range(3) for j in range(3)],
    )
    motion = [turned[pl.ds(9 + r, 8, stride=16), :] for r in range(3)]
    stress = {}
    for k in range(3):
        for m in range(k, 3):
            value = moved[k][0] * moved[m][0] + moved[k][1] * moved[m][1] + moved[k][2] * moved[m][2]
            stress[k, m] = stress[m, k] = value - 1.0 if k == m else value
    drag = [SPRING_RATE * (motion[k] - seen[k * 4]) for k in range(3)]
    for pair in range(4):
        lanes = slice(pair * 256, pair * 256 + 256)

        def row(x):
            return jnp.concatenate([x[2 * pair : 2 * pair + 1], x[2 * pair + 1 : 2 * pair + 2]], axis=1)

        for k in range(3):
            node_force = row(drag[k]) * shapes[0, :, lanes]
            for j in range(3):
                node_force = node_force - row(stress[k, j]) * shapes[1 + j, :, lanes]
            high, low = split(node_force)
            nodal[k * 64 : k * 64 + 64, lanes] = high
            nodal[192 + k * 64 : 192 + k * 64 + 64, lanes] = low
    force = dot_nt(nodal[...], onehot[...])
    for k in range(3):
        total = applied[k].reshape(64, 512)
        total = total - force[k * 64 : k * 64 + 64] - force[192 + k * 64 : 192 + k * 64 + 64]
        result = constrain(total, flipped, config_row)
        for y in range(4):
            fluid[pl.ds(k * 256 + y, 64, stride=4), :] = result[:, y * 128 : y * 128 + 128]

    arrive(reply_middle, reply_arrived, recvs.at[3])
    back_high, back_low = split(reply_arrived[...].reshape(128, 128).T)
    wide = dot(jnp.concatenate([back_high, back_low], axis=1), device_slot)
    slots = jnp.zeros((16, 1024), F32)
    for c in range(8):
        slots = slots + jnp.where(slot_place == c, wide[c * 16 : c * 16 + 16], 0.0)
    for g in range(8):
        grads[pl.ds(g, 16, stride=8), :] = slots[:, g * 128 : g * 128 + 128]
    moved = deformed(
        [items[r * 8 : r * 8 + 8, :] for r in range(9)],
        [grads[r * 8 : r * 8 + 8, :] for r in range(9)],
    )
    for k in range(3):
        for l in range(3):
            deform[(k * 3 + l) * 8 : (k * 3 + l) * 8 + 8, :] = moved[k][l]
    arrive(packet.at[0:15], middle.at[0:15], sends.at[0])
    arrive(reply.at[0:15], reply_middle.at[0:15], sends.at[1])
    arrive(middle.at[0:14], arrived.at[0:14], sends.at[2])
    arrive(reply_middle.at[0:14], reply_arrived.at[0:14], sends.at[3])
    arrive(sides_x, sides_x, sends.at[4])
    arrive(sides_y, sides_y, sends.at[5])
    arrive(sides_z, sides_z, sends.at[6])


def place_kernel(fluid, deform, fluid_hbm, deform_hbm, sem):
    copies = [
        pltpu.make_async_copy(fluid, fluid_hbm, sem.at[0]),
        pltpu.make_async_copy(deform, deform_hbm, sem.at[1]),
    ]
    for copy in copies:
        copy.start()
    for copy in copies:
        copy.wait()


def shards(velocity, viscosity, cell_config, constraint_offsets, slot_cells, point_coords, strain_offsets, solid_velocity):
    anywhere = pl.BlockSpec(memory_space=pl.ANY)
    inside = pl.BlockSpec(memory_space=pltpu.VMEM)
    vmem = pltpu.VMEM
    dma = pltpu.SemaphoreType.DMA
    fluid, deform = pl.pallas_call(
        kernel,
        out_shape=(vmem((768, 128), F32), vmem((72, 128), F32)),
        in_specs=[anywhere] * 8,
        out_specs=(inside, inside),
        scratch_shapes=[
            vmem((768, 128), F32),
            vmem((4, 128), F32),
            vmem((4, 128), jnp.int32),
            vmem((8, 64, 64), F32),
            vmem((8, 128), jnp.int32),
            vmem((128, 128), F32),
            vmem((1024, 128), BF16),
            vmem((3, 4, 16, 512), F32),
            vmem((384, 512), BF16),
            vmem((3, 4, 16, 512), F32),
            vmem((512, 1024), BF16),
            vmem((4, 64, 1024), F32),
            vmem((384, 1024), BF16),
            vmem((96, 128), F32),
            vmem((128, 128), F32),
            vmem((128, 128), F32),
            vmem((16, 8, 128), F32),
            vmem((16, 8, 128), F32),
            vmem((16, 8, 128), F32),
            vmem((16, 8, 128), F32),
            vmem((16, 8, 128), F32),
            vmem((16, 8, 128), F32),
            vmem((128, 128), F32),
            vmem((2, 8, 192), F32),
            vmem((2, 3, 16, 512), F32),
            vmem((2, 3, 4, 8, 128), F32),
            vmem((2, 8, 192), F32),
            dma((6,)),
            pltpu.SemaphoreType.REGULAR,
            pltpu.SemaphoreType.REGULAR((5,)),
            pltpu.SemaphoreType.REGULAR,
            dma((7,)),
            dma((7,)),
        ],
        compiler_params=pltpu.CompilerParams(collective_id=0, has_side_effects=True),
    )(
        velocity.reshape(768, 128),
        viscosity.reshape(4, 128),
        cell_config.reshape(4, 128),
        constraint_offsets,
        slot_cells.reshape(8, 128),
        point_coords.reshape(24, 128),
        strain_offsets.reshape(72, 128),
        solid_velocity.reshape(24, 128),
    )
    fluid, deform = pl.pallas_call(
        place_kernel,
        out_shape=(jax.ShapeDtypeStruct((768, 128), F32), jax.ShapeDtypeStruct((72, 128), F32)),
        in_specs=[inside, inside],
        out_specs=(anywhere, anywhere),
        scratch_shapes=[dma((2,))],
    )(pltpu.with_memory_space_constraint(fluid, pltpu.VMEM), pltpu.with_memory_space_constraint(deform, pltpu.VMEM))
    return fluid.reshape(velocity.shape), deform.reshape(strain_offsets.shape)


def solution(mesh):
    return jax.shard_map(
        shards,
        mesh=mesh,
        in_specs=(
            P(None, None, None, None, "dx", "dy", "solid"),
            P("dx", "dy", "solid"),
            P("dx", "dy", "solid"),
            P(),
            P("dx", ("dy", "solid"), None),
            P(None, "dx", ("dy", "solid"), None),
            P(None, None, "dx", ("dy", "solid"), None),
            P(None, "dx", ("dy", "solid"), None),
        ),
        out_specs=(
            P(None, None, None, None, "dx", "dy", "solid"),
            P(None, None, "dx", ("dy", "solid"), None),
        ),
        check_vma=False,
    )
```

```python
import jax
import jax.numpy as jnp
from jax import lax
from jax.experimental import pallas as pl
from jax.experimental.pallas import tpu as pltpu
from jax.sharding import PartitionSpec as P

F32 = jnp.float32
BF16 = jnp.bfloat16
TIME_STEP = 0.05
SPRING_RATE = 2.0
PENALTY = 4.0
NODE_POINTS = (0.0, 1.0 / 3.0, 2.0 / 3.0, 1.0)
N_DX, N_DY, N_SOLID = 4, 16, 8
MESH = pl.DeviceIdType.MESH


def iota(shape, dim):
    return lax.broadcasted_iota(jnp.int32, shape, dim)


def split(x):
    high = x.astype(BF16)
    return high, (x - high.astype(F32)).astype(BF16)


def dot(a, b):
    return lax.dot_general(a, b, (((1,), (0,)), ((), ())), preferred_element_type=F32)


def dot_nt(a, b):
    return lax.dot_general(a, b, (((1,), (1,)), ((), ())), preferred_element_type=F32)


def lagrange(coord):
    values = []
    slopes = []
    for which in range(4):
        others = [NODE_POINTS[j] for j in range(4) if j != which]
        denom = 1.0
        for other in others:
            denom = denom * (NODE_POINTS[which] - other)
        first = coord - others[0]
        second = coord - others[1]
        third = coord - others[2]
        scale = 1.0 / denom
        values.append(first * second * third * scale)
        slopes.append((second * third + first * third + first * second) * scale)
    return values, slopes


def pick(rows, index):
    out = jnp.where(index == 0, rows[0], rows[1])
    return jnp.where(index < 2, out, jnp.where(index == 2, rows[2], rows[3]))


def deformed(strain, grad):
    form = [[strain[k * 3 + l] + (1.0 if k == l else 0.0) for l in range(3)] for k in range(3)]
    return [
        [
            form[k][l]
            + TIME_STEP * (grad[k * 3] * form[0][l] + grad[k * 3 + 1] * form[1][l] + grad[k * 3 + 2] * form[2][l])
            for l in range(3)
        ]
        for k in range(3)
    ]


def stiffness():
    row, col = iota((64, 64), 0), iota((64, 64), 1)
    total = jnp.where(row == col, 6.0, 0.0)
    for step in (16, 4, 1):
        place_row, place_col = (row // step) % 4, (col // step) % 4
        same = (row - place_row * step) == (col - place_col * step)
        near = jnp.abs(place_row - place_col) == 1
        total = total - jnp.where(same & near, 1.0, 0.0)
    return total


def left_operand(stack):
    high, low = split(stack)
    return jnp.concatenate([high, high, low], axis=1)


def constrain(field, left, config):
    high, low = split(field)
    product = dot(left, jnp.concatenate([high, low, high], axis=0))
    total = field
    for which in range(8):
        total = total + jnp.where(config == which, product[which * 64 : which * 64 + 64], 0.0)
    return total


def kernel(
    vel_hbm, visc_hbm, config_hbm, offsets_hbm, cells_hbm, coords_hbm, strain_hbm, motion_hbm,
    fluid, deform,
    vel, visc, config, offsets, cells, items,
    slot_device, field, halves, applied, onehot, shapes, nodal, results, turned, grads,
    packet, middle, arrived, reply, reply_middle, reply_arrived, reply_turned,
    edge, sides_x, sides_y, sides_z,
    in_sem, entered_x, entered_y, entered_s, sends, recvs,
):
    me_x, me_y, me_s = lax.axis_index("dx"), lax.axis_index("dy"), lax.axis_index("solid")

    small_loads = [
        pltpu.make_async_copy(strain_hbm, items.at[0:72], in_sem.at[0]),
        pltpu.make_async_copy(motion_hbm, items.at[72:96], in_sem.at[0]),
        pltpu.make_async_copy(coords_hbm, items.at[96:120], in_sem.at[0]),
    ]
    loads = [
        pltpu.make_async_copy(cells_hbm, cells, in_sem.at[1]),
        pltpu.make_async_copy(vel_hbm, vel, in_sem.at[2]),
        pltpu.make_async_copy(offsets_hbm, offsets, in_sem.at[3]),
        pltpu.make_async_copy(config_hbm, config, in_sem.at[4]),
        pltpu.make_async_copy(visc_hbm, visc, in_sem.at[5]),
    ]
    for load in small_loads + loads:
        load.start()

    def rank(place):
        return jnp.where(place < 4, place, 11 - place)

    def later_s(step):
        return rank(lax.rem(me_s + step, N_SOLID)) > rank(me_s)

    barrier = pltpu.get_barrier_semaphore()
    for step in range(1, N_DY):

        @pl.when(me_y + step < N_DY)
        def _():
            pl.semaphore_signal(barrier, inc=1, device_id={"dy": me_y + step}, device_id_type=MESH)

    for step in range(1, N_SOLID):

        @pl.when(later_s(step))
        def _():
            pl.semaphore_signal(barrier, inc=1, device_id={"solid": lax.rem(me_s + step, N_SOLID)}, device_id_type=MESH)

    up_x, down_x = lax.rem(me_x + 1, N_DX), lax.rem(me_x + N_DX - 1, N_DX)
    for peer in (up_x, down_x):

        @pl.when(peer > me_x)
        def _():
            pl.semaphore_signal(barrier, inc=1, device_id={"dx": peer}, device_id_type=MESH)

    def over_solid(source, target, send, recv):
        copies = [pltpu.make_async_copy(source.at[:, me_s], target.at[:, me_s], recv)]
        for step in range(1, N_SOLID):
            peer = lax.rem(me_s + step, N_SOLID)
            copies.append(
                pltpu.make_async_remote_copy(
                    src_ref=source.at[:, peer],
                    dst_ref=target.at[:, me_s],
                    send_sem=send,
                    recv_sem=recv,
                    device_id={"solid": peer},
                    device_id_type=MESH,
                )
            )
        return copies

    def over_dy(source, target, send, recv):
        copies = [pltpu.make_async_copy(source.at[me_y], target.at[me_y], recv)]
        for step in range(1, N_DY):
            peer = lax.rem(me_y + step, N_DY)
            copies.append(
                pltpu.make_async_remote_copy(
                    src_ref=source.at[peer],
                    dst_ref=target.at[me_y],
                    send_sem=send,
                    recv_sem=recv,
                    device_id={"dy": peer},
                    device_id_type=MESH,
                )
            )
        return copies

    def start(copies):
        for copy in copies:
            copy.start()

    def start_early(copies):
        copies[0].start()
        for step in range(1, N_DY):

            @pl.when(me_y + step >= N_DY)
            def _():
                copies[step].start()

    def start_late(groups):
        for batch in range(5):
            later = jnp.clip(N_DY - 1 - me_y - 3 * batch, 0, 3)

            @pl.when(later > 0)
            def _():
                pl.semaphore_wait(entered_y.at[batch], later)

            for step in range(3 * batch + 1, 3 * batch + 4):

                @pl.when(me_y + step < N_DY)
                def _():
                    for copies in groups:
                        copies[step].start()

    def greet(entered, later):
        @pl.when(later > 0)
        def _():
            pl.semaphore_wait(entered, later)

    def arrive(source, target, recv):
        pltpu.make_async_copy(source, target, recv).wait()

    slot_place = iota((1, 1024), 1) & 7
    slot_device[...] = jnp.where((iota((1024, 128), 0) >> 3) == iota((1024, 128), 1), 1.0, 0.0).astype(BF16)
    reply_turned[...] = jnp.zeros_like(reply_turned)
    pltpu.make_async_copy(items.at[0:120], items.at[0:120], in_sem.at[0]).wait()
    loads[0].wait()
    items[120:128, :] = cells[...].astype(F32)
    rows = jnp.concatenate([items[pl.ds(g, 16, stride=8), :] for g in range(8)], axis=1)
    spread = jnp.concatenate([jnp.where(slot_place == c, rows, 0.0) for c in range(8)], axis=0)
    spread_high, spread_low = split(spread)
    packed = dot(spread_high, slot_device[...]) + dot(spread_low, slot_device[...])
    packet[...] = packed.T.reshape(16, 8, 128)
    turned[...] = packed

    earlier_x = jnp.where(me_x > 0, 1, 0) + jnp.where(me_x == N_DX - 1, 1, 0)
    earlier = me_y + rank(me_s) + earlier_x

    @pl.when(earlier > 0)
    def _():
        pl.semaphore_wait(barrier, earlier)

    first = over_dy(packet, middle, sends.at[0], recvs.at[0])
    start_early(first)
    for load in loads[1:]:
        load.wait()
    own_config = config[...]
    config_row = jnp.concatenate([own_config[y : y + 1] for y in range(4)], axis=1)
    left = left_operand(offsets[...].reshape(512, 64))
    points = [turned[pl.ds(12 + j, 8, stride=16), :] for j in range(3)]
    target = turned[pl.ds(15, 8, stride=16), :]
    polys = [lagrange(point) for point in points]
    cell_index = iota((512, 256), 0).astype(F32)
    node_row = iota((16, 256), 0)

    def tables(pair):
        lanes = slice(pair * 256, pair * 256 + 256)

        def row(x):
            return jnp.concatenate([x[2 * pair : 2 * pair + 1], x[2 * pair + 1 : 2 * pair + 2]], axis=1)

        onehot[:, lanes] = jnp.where(cell_index == row(target), 1.0, 0.0).astype(BF16)
        value_x, slope_x = [[row(x) for x in part] for part in polys[0]]
        value_y, slope_y = [pick([row(x) for x in part], node_row >> 2) for part in polys[1]]
        value_z, slope_z = [pick([row(x) for x in part], node_row & 3) for part in polys[2]]
        plain, along_y, along_z = value_y * value_z, slope_y * value_z, value_y * slope_z
        for a in range(4):
            at = slice(a * 16, a * 16 + 16)
            shapes[0, at, lanes] = value_x[a] * plain
            shapes[1, at, lanes] = slope_x[a] * plain
            shapes[2, at, lanes] = value_x[a] * along_y
            shapes[3, at, lanes] = value_x[a] * along_z

    for k in range(3):
        start_field = jnp.concatenate([vel[pl.ds(k * 256 + y, 64, stride=4), :] for y in range(4)], axis=1)
        own = constrain(start_field, left, config_row)
        field[k] = own.reshape(4, 16, 512)
        high, low = split(own)
        halves[k * 64 : k * 64 + 64] = high
        halves[192 + k * 64 : 192 + k * 64 + 64] = low
    for pair in range(4):
        tables(pair)
        lanes = slice(pair * 256, pair * 256 + 256)
        gathered = dot(halves[...], onehot[:, lanes])
        for k in range(3):
            nodes = gathered[k * 64 : k * 64 + 64] + gathered[192 + k * 64 : 192 + k * 64 + 64]
            for j in range(4):
                total = jnp.sum(nodes * shapes[j, :, lanes], axis=0, keepdims=True)
                line = (k * 4 + j) * 8 + 2 * pair
                results[line : line + 1, :] = total[:, :128]
                results[line + 1 : line + 2, :] = total[:, 128:]
    seen = [results[q * 8 : q * 8 + 8, :] for q in range(12)]
    for k in range(3):
        for j in range(3):
            reply_turned[pl.ds(k * 3 + j, 8, stride=16), :] = seen[k * 4 + 1 + j]
    reply[...] = reply_turned[...].T.reshape(16, 8, 128)
    second = over_dy(reply, reply_middle, sends.at[1], recvs.at[1])
    start_early(second)
    for step in range(1, N_DY):

        @pl.when(me_y >= step)
        def _():
            pl.semaphore_signal(entered_y.at[(step - 1) // 3], inc=1, device_id={"dy": me_y - step}, device_id_type=MESH)

    for step in range(1, N_SOLID):

        @pl.when(jnp.logical_not(later_s(step)))
        def _():
            pl.semaphore_signal(
                entered_s,
                inc=1,
                device_id={"solid": lax.rem(me_s + step, N_SOLID)},
                device_id_type=MESH,
            )

    for peer in (down_x, up_x):

        @pl.when(peer < me_x)
        def _():
            pl.semaphore_signal(entered_x, inc=1, device_id={"dx": peer}, device_id_type=MESH)


    def remote(source, target, which, where):
        return pltpu.make_async_remote_copy(
            src_ref=source, dst_ref=target, send_sem=sends.at[which], recv_sem=recvs.at[which],
            device_id=where, device_id_type=MESH,
        )

    up_y, down_y = lax.rem(me_y + 1, N_DY), lax.rem(me_y + N_DY - 1, N_DY)
    up_s, down_s = lax.rem(me_s + 1, N_SOLID), lax.rem(me_s + N_SOLID - 1, N_SOLID)
    halo = [
        remote(field.at[:, 3], sides_x.at[0], 4, {"dx": up_x}),
        remote(field.at[:, 0], sides_x.at[1], 4, {"dx": down_x}),
        remote(field.at[:, :, 8:16, 384:512], sides_y.at[0], 5, {"dy": up_y}),
        remote(field.at[:, :, 0:8, 0:128], sides_y.at[1], 5, {"dy": down_y}),
        remote(edge.at[0], sides_z.at[0], 6, {"solid": up_s}),
        remote(edge.at[1], sides_z.at[1], 6, {"solid": down_s}),
    ]
    edge_row, edge_col = iota((16, 512), 0), iota((16, 512), 1)
    lane_edge = jnp.where(edge_row < 8, 127, 0)
    edge_pick = jnp.where(
        (edge_col == (edge_row & 7) * 128 + lane_edge) & ((edge_row & 7) < 4), 1.0, 0.0
    ).astype(BF16)
    edges = dot_nt(edge_pick, halves[0:192]) + dot_nt(edge_pick, halves[192:384])
    edge[...] = edges.reshape(2, 8, 192)

    own_visc = visc[...]
    visc_row = jnp.concatenate([own_visc[y : y + 1] for y in range(4)], axis=1)
    stiff = stiffness().astype(BF16)
    stiff = jnp.concatenate([stiff, stiff], axis=1)
    node = iota((64, 512), 0)
    ends = jnp.zeros((64, 512), F32)
    for step in (16, 4, 1):
        place = (node // step) % 4
        ends = ends + jnp.where((place == 0) | (place == 3), PENALTY, 0.0)
    for k in range(3):
        both = jnp.concatenate([halves[k * 64 : k * 64 + 64], halves[192 + k * 64 : 192 + k * 64 + 64]], axis=0)
        own = field[k].reshape(64, 512)
        applied[k] = (own * (1.0 + ends) + visc_row * dot(stiff, both)).reshape(4, 16, 512)

    start_late([first, second])
    greet(entered_x, 2 - earlier_x)
    greet(entered_s, N_SOLID - 1 - rank(me_s))
    start(halo)
    arrive(packet, middle, recvs.at[0])
    third = over_solid(middle, arrived, sends.at[2], recvs.at[2])
    start(third)
    arrive(reply, reply_middle, recvs.at[1])
    fourth = over_solid(reply_middle, reply_arrived, sends.at[3], recvs.at[3])
    start(fourth)

    arrive(sides_x, sides_x, recvs.at[4])
    arrive(sides_y, sides_y, recvs.at[5])
    arrive(sides_z, sides_z, recvs.at[6])
    flipped = left_operand(jnp.concatenate([offsets[w].T for w in range(8)], axis=0))
    edge_lane = iota((32, 512), 1)
    edge_line = iota((32, 512), 0)
    edge_place = jnp.where(
        (edge_lane == (edge_line & 7) * 128 + jnp.where((edge_line & 8) == 0, 0, 127)) & ((edge_line & 7) < 4), 1.0, 0.0
    ).astype(BF16)
    below = jnp.where(me_s > 0, sides_z[0], 0.0)
    above = jnp.where(me_s < N_SOLID - 1, sides_z[1], 0.0)
    edge_high, edge_low = split(jnp.concatenate([below, above], axis=0).T)
    beside = dot(jnp.concatenate([edge_high, edge_low], axis=1), edge_place)
    lane = iota((64, 512), 1) & 127
    place_z = iota((64, 512), 0) & 3
    half_row = iota((4, 8, 512), 1)
    for k in range(3):
        own = field[k]
        flat = own.reshape(64, 512)
        outer = beside[k * 64 : k * 64 + 64]
        previous = jnp.concatenate([pltpu.roll(flat[:, y * 128 : y * 128 + 128], 1, 1) for y in range(4)], axis=1)
        following = jnp.concatenate([pltpu.roll(flat[:, y * 128 : y * 128 + 128], 127, 1) for y in range(4)], axis=1)
        previous = jnp.where(lane == 0, outer, previous)
        following = jnp.where(lane == 127, outer, following)
        near = jnp.where(place_z == 0, pltpu.roll(previous, 61, 0), 0.0)
        near = near + jnp.where(place_z == 3, pltpu.roll(following, 3, 0), 0.0)
        near = near.reshape(4, 16, 512)
        lower = jnp.concatenate([jnp.where(me_y > 0, sides_y[0, k], 0.0), own[:, 8:16, :384]], axis=2)
        upper = jnp.concatenate([own[:, 0:8, 128:], jnp.where(me_y < N_DY - 1, sides_y[1, k], 0.0)], axis=2)
        lower = jnp.where(half_row < 4, pltpu.roll(lower, 4, 1), 0.0)
        upper = jnp.where(half_row >= 4, pltpu.roll(upper, 4, 1), 0.0)
        near = near + jnp.concatenate([lower, upper], axis=1)
        lower = jnp.where(me_x > 0, sides_x[0, k], 0.0)[None]
        upper = jnp.where(me_x < N_DX - 1, sides_x[1, k], 0.0)[None]
        near = near + jnp.concatenate([lower, jnp.zeros((2, 16, 512), F32), upper], axis=0)
        applied[k] = applied[k] - PENALTY * near
    device_slot = jnp.where((iota((256, 1024), 1) >> 3) == (iota((256, 1024), 0) & 127), 1.0, 0.0).astype(BF16)

    arrive(middle, arrived, recvs.at[2])
    turned[...] = arrived[...].reshape(128, 128).T
    moved = deformed(
        [turned[pl.ds(r, 8, stride=16), :] for r in range(9)],
        [seen[k * 4 + 1 + j] for k in range(3) for j in range(3)],
    )
    motion = [turned[pl.ds(9 + r, 8, stride=16), :] for r in range(3)]
    stress = {}
    for k in range(3):
        for m in range(k, 3):
            value = moved[k][0] * moved[m][0] + moved[k][1] * moved[m][1] + moved[k][2] * moved[m][2]
            stress[k, m] = stress[m, k] = value - 1.0 if k == m else value
    drag = [SPRING_RATE * (motion[k] - seen[k * 4]) for k in range(3)]
    for pair in range(4):
        lanes = slice(pair * 256, pair * 256 + 256)

        def row(x):
            return jnp.concatenate([x[2 * pair : 2 * pair + 1], x[2 * pair + 1 : 2 * pair + 2]], axis=1)

        for k in range(3):
            node_force = row(drag[k]) * shapes[0, :, lanes]
            for j in range(3):
                node_force = node_force - row(stress[k, j]) * shapes[1 + j, :, lanes]
            high, low = split(node_force)
            nodal[k * 64 : k * 64 + 64, lanes] = high
            nodal[192 + k * 64 : 192 + k * 64 + 64, lanes] = low
    force = dot_nt(nodal[...], onehot[...])
    for k in range(3):
        total = applied[k].reshape(64, 512)
        total = total - force[k * 64 : k * 64 + 64] - force[192 + k * 64 : 192 + k * 64 + 64]
        result = constrain(total, flipped, config_row)
        for y in range(4):
            fluid[pl.ds(k * 256 + y, 64, stride=4), :] = result[:, y * 128 : y * 128 + 128]

    arrive(reply_middle, reply_arrived, recvs.at[3])
    back_high, back_low = split(reply_arrived[...].reshape(128, 128).T)
    wide = dot(jnp.concatenate([back_high, back_low], axis=1), device_slot)
    slots = jnp.zeros((16, 1024), F32)
    for c in range(8):
        slots = slots + jnp.where(slot_place == c, wide[c * 16 : c * 16 + 16], 0.0)
    for g in range(8):
        grads[pl.ds(g, 16, stride=8), :] = slots[:, g * 128 : g * 128 + 128]
    moved = deformed(
        [items[r * 8 : r * 8 + 8, :] for r in range(9)],
        [grads[r * 8 : r * 8 + 8, :] for r in range(9)],
    )
    for k in range(3):
        for l in range(3):
            deform[(k * 3 + l) * 8 : (k * 3 + l) * 8 + 8, :] = moved[k][l]
    arrive(packet.at[0:15], middle.at[0:15], sends.at[0])
    arrive(reply.at[0:15], reply_middle.at[0:15], sends.at[1])
    arrive(middle.at[0:14], arrived.at[0:14], sends.at[2])
    arrive(reply_middle.at[0:14], reply_arrived.at[0:14], sends.at[3])
    arrive(sides_x, sides_x, sends.at[4])
    arrive(sides_y, sides_y, sends.at[5])
    arrive(sides_z, sides_z, sends.at[6])


def place_kernel(fluid, deform, fluid_hbm, deform_hbm, sem):
    copies = [
        pltpu.make_async_copy(fluid, fluid_hbm, sem.at[0]),
        pltpu.make_async_copy(deform, deform_hbm, sem.at[1]),
    ]
    for copy in copies:
        copy.start()
    for copy in copies:
        copy.wait()


def shards(velocity, viscosity, cell_config, constraint_offsets, slot_cells, point_coords, strain_offsets, solid_velocity):
    anywhere = pl.BlockSpec(memory_space=pl.ANY)
    inside = pl.BlockSpec(memory_space=pltpu.VMEM)
    vmem = pltpu.VMEM
    dma = pltpu.SemaphoreType.DMA
    fluid, deform = pl.pallas_call(
        kernel,
        out_shape=(vmem((768, 128), F32), vmem((72, 128), F32)),
        in_specs=[anywhere] * 8,
        out_specs=(inside, inside),
        scratch_shapes=[
            vmem((768, 128), F32),
            vmem((4, 128), F32),
            vmem((4, 128), jnp.int32),
            vmem((8, 64, 64), F32),
            vmem((8, 128), jnp.int32),
            vmem((128, 128), F32),
            vmem((1024, 128), BF16),
            vmem((3, 4, 16, 512), F32),
            vmem((384, 512), BF16),
            vmem((3, 4, 16, 512), F32),
            vmem((512, 1024), BF16),
            vmem((4, 64, 1024), F32),
            vmem((384, 1024), BF16),
            vmem((96, 128), F32),
            vmem((128, 128), F32),
            vmem((128, 128), F32),
            vmem((16, 8, 128), F32),
            vmem((16, 8, 128), F32),
            vmem((16, 8, 128), F32),
            vmem((16, 8, 128), F32),
            vmem((16, 8, 128), F32),
            vmem((16, 8, 128), F32),
            vmem((128, 128), F32),
            vmem((2, 8, 192), F32),
            vmem((2, 3, 16, 512), F32),
            vmem((2, 3, 4, 8, 128), F32),
            vmem((2, 8, 192), F32),
            dma((6,)),
            pltpu.SemaphoreType.REGULAR,
            pltpu.SemaphoreType.REGULAR((5,)),
            pltpu.SemaphoreType.REGULAR,
            dma((7,)),
            dma((7,)),
        ],
        compiler_params=pltpu.CompilerParams(collective_id=0, has_side_effects=True),
    )(
        velocity.reshape(768, 128),
        viscosity.reshape(4, 128),
        cell_config.reshape(4, 128),
        constraint_offsets,
        slot_cells.reshape(8, 128),
        point_coords.reshape(24, 128),
        strain_offsets.reshape(72, 128),
        solid_velocity.reshape(24, 128),
    )
    fluid, deform = pl.pallas_call(
        place_kernel,
        out_shape=(jax.ShapeDtypeStruct((768, 128), F32), jax.ShapeDtypeStruct((72, 128), F32)),
        in_specs=[inside, inside],
        out_specs=(anywhere, anywhere),
        scratch_shapes=[dma((2,))],
    )(pltpu.with_memory_space_constraint(fluid, pltpu.VMEM), pltpu.with_memory_space_constraint(deform, pltpu.VMEM))
    return fluid.reshape(velocity.shape), deform.reshape(strain_offsets.shape)


def solution(mesh):
    return jax.shard_map(
        shards,
        mesh=mesh,
        in_specs=(
            P(None, None, None, None, "dx", "dy", "solid"),
            P("dx", "dy", "solid"),
            P("dx", "dy", "solid"),
            P(),
            P("dx", ("dy", "solid"), None),
            P(None, "dx", ("dy", "solid"), None),
            P(None, None, "dx", ("dy", "solid"), None),
            P(None, "dx", ("dy", "solid"), None),
        ),
        out_specs=(
            P(None, None, None, None, "dx", "dy", "solid"),
            P(None, None, "dx", ("dy", "solid"), None),
        ),
        check_vma=False,
    )
```
